256 devices in a mesh: row: 16 (over z_lo, x, core), col: 16 (over y, z_hi).
Axes of the slice: x: 4, y: 4, z: 8 (z_hi: 4, z_lo: 2; z = z_hi * 2 + z_lo), core: 2. Of those that a mesh axis runs over, the one named last changes fastest.
Arguments:
- object_field: float32 [2, 8192, 8192], P(None, 'row', 'col'), may hold values from -5 to 5
- probe: float32 [2, 256, 256], replicated, may hold values from -5 to 5
- amplitude: float32 [16, 16, 8, 256, 256], P('row', 'col'), may hold values from 0.2 to 3
- offsets: int32 [16, 16, 8, 2], P('row', 'col'), may hold values from 0 to 511
Outputs:
- object_grad: float32 [2, 8192, 8192], P(None, 'row', 'col')
- probe_grad: float32 [2, 256, 256], replicated
The draws below stay inside these ranges and needn't reach their ends.
All inputs are finite; a program needn't handle non-finite values.
Results may differ from the reference program's by a relative error of at most 0.0003.
Values sent between devices are 32-bit elements; how exact they have to be, the bound alone decides.
No kernel may reach another device: no remote copies, remote signals or barrier semaphores. Data moves between devices by JAX's collectives and lax.ppermute only.
A program may use at most 64 MiB of HBM per device.

```python
import math
import jax
import jax.numpy as jnp
from jax import lax

PS = 256
TILE = 512
PATCHES = 8
GRID_R = 16
GRID_C = 16
NR = 8192
NC = 8192


def with_ends(entries, rng, least, top_value):
    extent = entries.shape
    index_at = [jax.random.randint(jax.random.fold_in(rng, axis), (), 0, extent[axis]) for axis in range(len(extent))]
    entries = entries.at[tuple(index_at)].set(least)
    longest = extent.index(max(extent))
    index_at[longest] = (index_at[longest] + 1) % extent[longest]
    return entries.at[tuple(index_at)].set(top_value)


def levels(own_key, extent, shards, low, top_value):
    loudness, own = 1.0, jax.random.fold_in(own_key, 6)
    for axis_at, shards_of in shards:
        draws = jnp.exp(jax.random.uniform(jax.random.fold_in(own, axis_at), (shards_of,), jnp.float32, low / len(shards), top_value / len(shards)))
        loudness = loudness * jnp.repeat(draws, extent[axis_at] // shards_of).reshape([-1 if axis == axis_at else 1 for axis in range(len(extent))])
    return loudness


def noise(rng, dims, width, reach, shards=(), kind=jnp.bfloat16):
    array = jax.random.normal(rng, dims, jnp.float32) * width
    if len(shards) > 0:
        array = levels(rng, dims, shards, -0.22, 0.18) * array
    return jnp.clip(array, min=-reach, max=reach).astype(kind)


def setup_inputs(seed: int = 0) -> dict:
    splits = jax.random.split(jax.random.key(seed), 5)
    object_field = noise(splits[0], (2, NR, NC), 0.7, 5.0, ((1, 16), (2, 16)), jnp.float32)
    probe = noise(splits[1], (2, PS, PS), 0.7, 5.0, (), jnp.float32)
    amplitude = jnp.clip(jnp.exp(math.log(3.0) - 2.7080502 * jax.random.uniform(splits[2], (GRID_R, GRID_C, PATCHES, PS, PS), jnp.float32) ** levels(splits[2], (GRID_R, GRID_C, PATCHES, PS, PS), ((0, 16), (1, 16)), -0.2, 0.2)), 0.2, 3.0)
    offsets = with_ends(jax.random.randint(splits[3], (GRID_R, GRID_C, PATCHES, 2), 0, TILE), jax.random.fold_in(splits[3], 1), 0, TILE - 1).astype(jnp.int32)
    return dict(object_field=object_field, probe=probe, amplitude=amplitude, offsets=offsets)


def tables(size):
    index = jnp.arange(size, dtype=jnp.int32)
    product = index[:, None] * index[None, :] % size
    angle = product.astype(jnp.float32) * (2.0 * math.pi / size)
    scale = 1.0 / math.sqrt(size)
    return (jnp.cos(angle) * scale, jnp.sin(angle) * scale)

def matmul(left, right):
    return jnp.dot(left, right, precision=lax.Precision.HIGHEST, preferred_element_type=jnp.float32)

def transform(real_part, imag_part, cosine, sine, sign):
    left_r = matmul(cosine, real_part) - sign * matmul(sine, imag_part)
    left_i = matmul(cosine, imag_part) + sign * matmul(sine, real_part)
    out_r = matmul(left_r, cosine) - sign * matmul(left_i, sine)
    out_i = matmul(left_i, cosine) + sign * matmul(left_r, sine)
    return (out_r, out_i)

def patch_terms(view, probe, amp, cosine, sine):
    probe_r, probe_i = (probe[0], probe[1])
    view_r, view_i = (view[0], view[1])
    wave_r = probe_r * view_r - probe_i * view_i
    wave_i = probe_r * view_i + probe_i * view_r
    far_r, far_i = transform(wave_r, wave_i, cosine, sine, -1.0)
    modulus = jnp.sqrt(far_r * far_r + far_i * far_i)
    keep = 1.0 - amp / jnp.maximum(modulus, 0.5)
    chi_r, chi_i = transform(far_r * keep, far_i * keep, cosine, sine, 1.0)
    obj_term = jnp.stack([probe_r * chi_r + probe_i * chi_i, probe_r * chi_i - probe_i * chi_r])
    probe_term = jnp.stack([view_r * chi_r + view_i * chi_i, view_r * chi_i - view_i * chi_r])
    return (obj_term, probe_term)

def reference(object_field, probe, amplitude, offsets):
    cosine, sine = tables(PS)
    padded = jnp.pad(object_field, ((0, 0), (0, PS), (0, PS)))
    flat_off = offsets.reshape(-1, 2).astype(jnp.int32)
    flat_amp = amplitude.reshape(-1, PS, PS)
    count = GRID_R * GRID_C * PATCHES
    numbers = jnp.arange(count, dtype=jnp.int32)

    def step(carry, item):
        grad, probe_acc = carry
        number, off, amp = item
        tile_r = number // (GRID_C * PATCHES)
        tile_c = number // PATCHES % GRID_C
        top = (tile_r * TILE + off[0]).astype(jnp.int32)
        left = (tile_c * TILE + off[1]).astype(jnp.int32)
        zero = jnp.zeros((), jnp.int32)
        view = lax.dynamic_slice(padded, (zero, top, left), (2, PS, PS))
        obj_term, probe_term = patch_terms(view, probe, amp, cosine, sine)
        old = lax.dynamic_slice(grad, (zero, top, left), (2, PS, PS))
        grad = lax.dynamic_update_slice(grad, old + obj_term, (zero, top, left))
        return ((grad, probe_acc + probe_term), None)
    start = (jnp.zeros(padded.shape, jnp.float32), jnp.zeros((2, PS, PS), jnp.float32))
    (grad, probe_acc), _ = lax.scan(step, start, (numbers, flat_off, flat_amp))
    return (grad[:, :NR, :NC], probe_acc / count)
```

```python
import functools
import math

import jax
import jax.numpy as jnp
import numpy as np
from jax import lax
from jax.experimental import pallas as pl
from jax.experimental.pallas import tpu as pltpu
from jax.sharding import PartitionSpec as P

F32 = jnp.float32
BF16 = jnp.bfloat16


def passed_along(value, axis, steps):
    count = lax.axis_size(axis)
    first, last = (max(0, -steps), min(count, count - steps))
    return lax.ppermute(value, axis, [(source, source + steps) for source in range(first, last)])


def split(value):
    high = value.astype(BF16)
    return high, (value - high.astype(F32)).astype(BF16)


def dft_tables(size):
    index = np.arange(size)
    angle = (index[:, None] * index[None, :] % size) * (2.0 * math.pi / size)
    cosine = (np.cos(angle) / math.sqrt(size)).astype(np.float32)
    sine = (np.sin(angle) / math.sqrt(size)).astype(np.float32)
    forward = np.concatenate([np.concatenate([cosine, -sine], 1), np.concatenate([sine, cosine], 1)], 0)
    backward = np.concatenate([np.concatenate([cosine, sine], 1), np.concatenate([-sine, cosine], 1)], 0)
    stacked = np.concatenate([cosine, sine], 0)
    return stacked, forward, backward


def dot(left, right):
    return jnp.dot(left, right, preferred_element_type=F32)


def dot3(left, right):
    return dot(left[0], right[0]) + (dot(left[0], right[1]) + dot(left[1], right[0]))


def both_sides(real_part, imag_part, stacked, wide, sign):
    side = real_part.shape[0]
    columns = split(jnp.concatenate([real_part, imag_part], axis=1))
    product = dot3(stacked, columns)
    cos_r, cos_i = product[:side, :side], product[:side, side:]
    sin_r, sin_i = product[side:, :side], product[side:, side:]
    left = split(jnp.concatenate([cos_r - sign * sin_i, cos_i + sign * sin_r], axis=1))
    out = dot3(left, wide)
    return out[:, :side], out[:, side:]


def patches_kernel(off, tile, right, bottom, corner, probe, amp, stacked, forward, backward,
                   main_out, right_out, bottom_out, corner_out, probe_out, ext, grad):
    side = probe.shape[1]
    rows, cols = tile.shape[1], tile.shape[2]
    ext[:, :rows, :cols] = tile[...]
    ext[:, :rows, cols:] = right[...]
    ext[:, rows:, :cols] = bottom[...]
    ext[:, rows:, cols:] = corner[...]
    grad[...] = jnp.zeros_like(grad)
    probe_out[...] = jnp.zeros_like(probe_out)

    def step(number, carry):
        top = off[number, 0]
        left = off[number, 1]
        row_base = pl.multiple_of(top // 8 * 8, 8)
        base = pl.multiple_of(left // 128 * 128, 128)
        row = top - row_base
        lane = left - base
        tall, span = side + 8, side + 128
        up = lax.rem(tall - row, tall)
        back = lax.rem(span - lane, span)
        pr, pi = probe[0], probe[1]

        def window(part):
            block = ext[part, pl.ds(row_base, tall), pl.ds(base, span)]
            return pltpu.roll(pltpu.roll(block, back, 1)[:, :side], up, 0)[:side]

        vr, vi = window(0), window(1)
        fr, fi = both_sides(pr * vr - pi * vi, pr * vi + pi * vr,
                            (stacked[0], stacked[1]), (forward[0], forward[1]), -1.0)
        keep = 1.0 - amp[number] * lax.rsqrt(jnp.maximum(fr * fr + fi * fi, 0.25))
        cr, ci = both_sides(fr * keep, fi * keep,
                            (stacked[0], stacked[1]), (backward[0], backward[1]), 1.0)
        vr, vi = window(0), window(1)
        probe_out[0] += vr * cr + vi * ci
        probe_out[1] += vr * ci - vi * cr
        below = jnp.zeros((8, side), F32)
        beside = jnp.zeros((tall, 128), F32)

        def add(part, term):
            moved = pltpu.roll(jnp.concatenate([term, below], axis=0), row, 0)
            moved = pltpu.roll(jnp.concatenate([moved, beside], axis=1), lane, 1)
            grad[part, pl.ds(row_base, tall), pl.ds(base, span)] += moved

        add(0, pr * cr + pi * ci)
        add(1, pr * ci - pi * cr)
        return carry

    lax.fori_loop(0, amp.shape[0], step, 0)
    main_out[...] = grad[:, :rows, :cols]
    right_out[...] = grad[:, :rows, cols:]
    bottom_out[...] = grad[:, rows:, :cols]
    corner_out[...] = grad[:, rows:, cols:]


def all_patches(off, tile, right, bottom, corner, probe, amp):
    side = probe.shape[1]
    rows, cols = tile.shape[1], tile.shape[2]
    tables = [jnp.stack(split(jnp.asarray(table))) for table in dft_tables(side)]
    vmem = pl.BlockSpec(memory_space=pltpu.VMEM)
    shape = lambda *dims: jax.ShapeDtypeStruct(dims, F32)
    return pl.pallas_call(
        patches_kernel,
        out_shape=(shape(2, rows, cols), shape(2, rows, side), shape(2, side, cols),
                   shape(2, side, side), shape(2, side, side)),
        in_specs=[pl.BlockSpec(memory_space=pltpu.SMEM)] + [vmem] * 9,
        out_specs=[vmem] * 5,
        scratch_shapes=[pltpu.VMEM((2, rows + side, cols + side), F32),
                        pltpu.VMEM((2, rows + side, cols + side), F32)],
        compiler_params=pltpu.CompilerParams(vmem_limit_bytes=60 * 1024 * 1024),
    )(off, tile, right, bottom, corner, probe, amp, *tables)


def halving_sum(value):
    shape = value.shape
    value = value.reshape(-1, 128)
    steps = [("row", bit) for bit in (1, 2, 4, 8)] + [("col", bit) for bit in (4, 8, 1, 2)]
    for axis, bit in steps:
        upper = (lax.axis_index(axis) & bit) != 0
        half = value.shape[0] // 2
        low, high = value[:half], value[half:]
        pairs = [(i, i ^ bit) for i in range(lax.axis_size(axis))]
        got = lax.ppermute(jnp.where(upper, low, high), axis, pairs)
        value = jnp.where(upper, high, low) + got
    for axis, bit in reversed(steps):
        upper = (lax.axis_index(axis) & bit) != 0
        pairs = [(i, i ^ bit) for i in range(lax.axis_size(axis))]
        got = lax.ppermute(value, axis, pairs)
        value = jnp.concatenate([jnp.where(upper, got, value), jnp.where(upper, value, got)], 0)
    return value.reshape(shape)


def shards(object_field, probe, amplitude, offsets):
    side = probe.shape[1]
    right = passed_along(object_field[:, :, :side], "col", -1)
    bottom = passed_along(object_field[:, :side, :], "row", -1)
    corner = passed_along(right[:, :side, :], "row", -1)
    main, right, bottom, corner, probe_acc = all_patches(
        offsets[0, 0], object_field, right, bottom, corner, probe, amplitude[0, 0])
    corner_back = passed_along(corner, "row", 1)
    bottom_back = passed_along(bottom, "row", 1)
    right = right.at[:, :side, :].add(corner_back)
    right_back = passed_along(right, "col", 1)
    count = amplitude.shape[2] * lax.axis_size("row") * lax.axis_size("col")
    probe_total = halving_sum(probe_acc) / count
    main = main.at[:, :side, :].add(bottom_back)
    object_grad = main.at[:, :, :side].add(right_back)
    return (object_grad, probe_total)


def solution(mesh):
    placed = (
        P(None, "row", "col"),
        P(),
        P("row", "col", None, None, None),
        P("row", "col", None, None),
    )
    return jax.shard_map(
        shards, mesh=mesh, in_specs=placed, out_specs=(P(None, "row", "col"), P()), check_vma=False
    )
```

```python
import math

import jax
import jax.numpy as jnp
import numpy as np
from jax import lax
from jax.experimental import pallas as pl
from jax.experimental.pallas import tpu as pltpu
from jax.sharding import PartitionSpec as P


F32 = jnp.float32
BF16 = jnp.bfloat16


def passed_along(value, axis, steps):
    count = lax.axis_size(axis)
    first, last = (max(0, -steps), min(count, count - steps))
    return lax.ppermute(value, axis, [(source, source + steps) for source in range(first, last)])


def split(value):
    high = value.astype(BF16)
    return high, (value - high.astype(F32)).astype(BF16)


def dft_tables(size):
    index = np.arange(size)
    angle = (index[:, None] * index[None, :] % size) * (2.0 * math.pi / size)
    cosine = (np.cos(angle) / math.sqrt(size)).astype(np.float32)
    sine = (np.sin(angle) / math.sqrt(size)).astype(np.float32)
    forward = np.concatenate([np.concatenate([cosine, -sine], 1), np.concatenate([sine, cosine], 1)], 0)
    backward = np.concatenate([np.concatenate([cosine, sine], 1), np.concatenate([-sine, cosine], 1)], 0)
    stacked = np.concatenate([cosine, sine], 0)
    return stacked, forward, backward


def dot(left, right):
    return jnp.dot(left, right, preferred_element_type=F32)


def dot3(left, right):
    return dot(left[0], right[0]) + (dot(left[0], right[1]) + dot(left[1], right[0]))


def both_sides(real_part, imag_part, stacked, wide, sign):
    side = real_part.shape[0]
    columns = split(jnp.concatenate([real_part, imag_part], axis=1))
    product = dot3(stacked, columns)
    cos_r, cos_i = product[:side, :side], product[:side, side:]
    sin_r, sin_i = product[side:, :side], product[side:, side:]
    left = split(jnp.concatenate([cos_r - sign * sin_i, cos_i + sign * sin_r], axis=1))
    out = dot3(left, wide)
    return out[:, :side], out[:, side:]


def patches_kernel(off, tile, right, bottom, corner, probe, amp, stacked, forward, backward,
                   main_out, upper_out, lower_out, bottom_out, corner_out, probe_out, ext, grad):
    side = probe.shape[1]
    rows, cols = tile.shape[1], tile.shape[2]
    ext[:, :rows, :cols] = tile[...]
    ext[:, :rows, cols:] = right[...]
    ext[:, rows:, :cols] = bottom[...]
    ext[:, rows:, cols:] = corner[...]
    grad[...] = jnp.zeros_like(grad)
    probe_out[...] = jnp.zeros_like(probe_out)

    def step(number, carry):
        top = off[number, 0]
        left = off[number, 1]
        row_base = pl.multiple_of(top // 8 * 8, 8)
        base = pl.multiple_of(left // 128 * 128, 128)
        row = top - row_base
        lane = left - base
        tall, span = side + 8, side + 128
        up = lax.rem(tall - row, tall)
        back = lax.rem(span - lane, span)
        pr, pi = probe[0], probe[1]

        def window(part):
            block = ext[part, pl.ds(row_base, tall), pl.ds(base, span)]
            return pltpu.roll(pltpu.roll(block, back, 1)[:, :side], up, 0)[:side]

        vr, vi = window(0), window(1)
        fr, fi = both_sides(pr * vr - pi * vi, pr * vi + pi * vr,
                            (stacked[0], stacked[1]), (forward[0], forward[1]), -1.0)
        keep = 1.0 - amp[number] * lax.rsqrt(jnp.maximum(fr * fr + fi * fi, 0.25))
        cr, ci = both_sides(fr * keep, fi * keep,
                            (stacked[0], stacked[1]), (backward[0], backward[1]), 1.0)
        vr, vi = window(0), window(1)
        probe_out[0] += vr * cr + vi * ci
        probe_out[1] += vr * ci - vi * cr
        below = jnp.zeros((8, side), F32)
        beside = jnp.zeros((tall, 128), F32)

        def add(part, term):
            moved = pltpu.roll(jnp.concatenate([term, below], axis=0), row, 0)
            moved = pltpu.roll(jnp.concatenate([moved, beside], axis=1), lane, 1)
            grad[part, pl.ds(row_base, tall), pl.ds(base, span)] += moved

        add(0, pr * cr + pi * ci)
        add(1, pr * ci - pi * cr)
        return carry

    lax.fori_loop(0, amp.shape[0], step, 0)
    main_out[...] = grad[:, :rows, :cols]
    upper_out[...] = grad[:, :side, cols:]
    lower_out[...] = grad[:, side:rows, cols:]
    bottom_out[...] = grad[:, rows:, :cols]
    corner_out[...] = grad[:, rows:, cols:]


def all_patches(off, tile, right, bottom, corner, probe, amp):
    side = probe.shape[1]
    rows, cols = tile.shape[1], tile.shape[2]
    tables = [jnp.stack(split(jnp.asarray(table))) for table in dft_tables(side)]
    vmem = pl.BlockSpec(memory_space=pltpu.VMEM)
    shape = lambda *dims: jax.ShapeDtypeStruct(dims, F32)
    return pl.pallas_call(
        patches_kernel,
        out_shape=(shape(2, rows, cols), shape(2, side, side), shape(2, rows - side, side), shape(2, side, cols),
                   shape(2, side, side), shape(2, side, side)),
        in_specs=[pl.BlockSpec(memory_space=pltpu.SMEM)] + [vmem] * 9,
        out_specs=[vmem] * 6,
        scratch_shapes=[pltpu.VMEM((2, rows + side, cols + side), F32),
                        pltpu.VMEM((2, rows + side, cols + side), F32)],
        compiler_params=pltpu.CompilerParams(vmem_limit_bytes=26 * 1024 * 1024),
    )(off, tile, right, bottom, corner, probe, amp, *tables)


HALVED = (("row", 1), ("row", 2), ("row", 4), ("col", 4))
WHOLE = (("col", 8), ("row", 8), ("col", 1), ("col", 2))


def swapped(value, axis, bit):
    return lax.ppermute(value, axis, [(i, i ^ bit) for i in range(lax.axis_size(axis))])


def summed_everywhere(value):
    shape = value.shape
    value = value.reshape(-1, 128)
    for axis, bit in HALVED:
        upper = (lax.axis_index(axis) & bit) != 0
        half = value.shape[0] // 2
        low, high = value[:half], value[half:]
        got = swapped(jnp.where(upper, low, high), axis, bit)
        value = jnp.where(upper, high, low) + got
    for axis, bit in WHOLE:
        value = value + swapped(value, axis, bit)
    for axis, bit in reversed(HALVED):
        upper = (lax.axis_index(axis) & bit) != 0
        got = swapped(value, axis, bit)
        value = jnp.concatenate([jnp.where(upper, got, value), jnp.where(upper, value, got)], 0)
    return value.reshape(shape)


def shards_body(object_field, probe, amplitude, offsets):
    side = probe.shape[1]
    right = passed_along(object_field[:, :, :side], "col", -1)
    bottom = passed_along(object_field[:, :side, :], "row", -1)
    corner = passed_along(right[:, :side, :], "row", -1)
    main, upper, lower, bottom, corner, probe_acc = all_patches(
        offsets[0, 0], object_field, right, bottom, corner, probe, amplitude[0, 0])
    corner_back = passed_along(corner, "row", 1)
    lower_back = passed_along(lower, "col", 1)
    bottom_back = passed_along(bottom, "row", 1)
    upper_back = passed_along(upper + corner_back, "col", 1)
    count = amplitude.shape[2] * lax.axis_size("row") * lax.axis_size("col")
    probe_total = summed_everywhere(probe_acc) / count
    right_back = jnp.concatenate([upper_back, lower_back], axis=1)
    main = main.at[:, :side, :].add(bottom_back)
    object_grad = main.at[:, :, :side].add(right_back)
    return (object_grad, probe_total)


def solution(mesh):
    placed = (
        P(None, "row", "col"),
        P(),
        P("row", "col", None, None, None),
        P("row", "col", None, None),
    )
    return jax.shard_map(
        shards_body, mesh=mesh, in_specs=placed, out_specs=(P(None, "row", "col"), P()), check_vma=False
    )
```

```python
import math

import jax
import jax.numpy as jnp
import numpy as np
from jax import lax
from jax.experimental import pallas as pl
from jax.experimental.pallas import tpu as pltpu
from jax.sharding import PartitionSpec as P


F32 = jnp.float32
BF16 = jnp.bfloat16


def passed_along(value, axis, steps):
    count = lax.axis_size(axis)
    first, last = (max(0, -steps), min(count, count - steps))
    return lax.ppermute(value, axis, [(source, source + steps) for source in range(first, last)])


def split(value):
    high = value.astype(BF16)
    return high, (value - high.astype(F32)).astype(BF16)


def half_tables(size):
    half = size // 2
    tables = []
    for odd in (0, 1):
        angle = ((2 * np.arange(half)[:, None] + odd) * np.arange(half)[None, :] % size) * (2.0 * math.pi / size)
        cosine, sine = np.cos(angle) / math.sqrt(size), np.sin(angle) / math.sqrt(size)
        tables.append(np.block([[cosine, sine], [-sine, cosine]]).astype(np.float32))
    return np.stack(tables)


def split_table(table):
    high = table.astype(BF16)
    return np.stack([high, (table - high.astype(np.float32)).astype(BF16)], axis=1)


def dot(left, right):
    return jnp.dot(left, right, preferred_element_type=F32)


def rolled(block, shift, axis):
    size = block.shape[axis]
    small = 8 if axis == 0 else 128
    count = size // small
    pieces = []
    for index in range(count):
        piece = block[index * small:(index + 1) * small] if axis == 0 else block[:, index * small:(index + 1) * small]
        pieces.append(pltpu.roll(piece, shift, axis))
    place = lax.broadcasted_iota(jnp.int32, pieces[0].shape, axis)
    inside = place >= shift
    out = [jnp.where(inside, pieces[index], pieces[index - 1]) for index in range(count)]
    return jnp.concatenate(out, axis=axis)


def unrolled(block, shift, axis):
    size = block.shape[axis]
    small = 8 if axis == 0 else 128
    count = size // small
    back = lax.rem(small - shift, small)
    pieces = []
    for index in range(count):
        piece = block[index * small:(index + 1) * small] if axis == 0 else block[:, index * small:(index + 1) * small]
        pieces.append(pltpu.roll(piece, back, axis))
    place = lax.broadcasted_iota(jnp.int32, pieces[0].shape, axis)
    inside = place < small - shift
    out = [jnp.where(inside, pieces[index], pieces[(index + 1) % count]) for index in range(count)]
    return jnp.concatenate(out, axis=axis)


def prepare_kernel(off, amp, probe, pick, amp_out, probe_out):
    number = pl.program_id(0)
    side = probe.shape[1]
    half = side // 2
    row, lane = lax.rem(off[number, 0], 8), lax.rem(off[number, 1], 128)
    high, low = split(amp[0])
    high, low = split(dot(high, pick[0]) + dot(low, pick[0]))
    both = dot(pick[1], high) + dot(pick[1], low)
    amp_out[0, 0] = both[:, :half]
    amp_out[0, 1] = both[:, half:]
    for part in (0, 1):
        probe_out[0, part] = rolled(rolled(probe[part], row, 0), lane, 1)


def prepare(off, amp, probe):
    count, side = amp.shape[0], amp.shape[1]
    half = side // 2
    pick = np.zeros((side, side), np.float32)
    pick[2 * np.arange(half), np.arange(half)] = 1.0
    pick[2 * np.arange(half) + 1, half + np.arange(half)] = 1.0
    return pl.pallas_call(
        prepare_kernel,
        grid=(count,),
        out_shape=(jax.ShapeDtypeStruct((count, 2, side, half), F32), jax.ShapeDtypeStruct((count, 2, side, side), F32)),
        in_specs=[pl.BlockSpec(memory_space=pltpu.SMEM),
                  pl.BlockSpec((1, side, side), lambda i: (i, 0, 0)),
                  pl.BlockSpec((2, side, side), lambda i: (0, 0, 0)),
                  pl.BlockSpec((2, side, side), lambda i: (0, 0, 0))],
        out_specs=(pl.BlockSpec((1, 2, side, half), lambda i: (i, 0, 0, 0)),
                   pl.BlockSpec((1, 2, side, side), lambda i: (i, 0, 0, 0))),
    )(off, amp, probe, jnp.asarray(np.stack([pick, pick.T]).astype(BF16)))


def one_patch(top, left, amp, probe, left_table, right_table, ext, grad, probe_acc,
              view, a_high, a_low, x_high, x_low):
    side = probe.shape[1]
    half, step = side // 2, 32
    base_row = pl.multiple_of(top // 8 * 8, 8)
    base_col = pl.multiple_of(left // 128 * 128, 128)
    row, lane = top - base_row, left - base_col
    lanes = lax.broadcasted_iota(jnp.int32, (8, 128), 1)
    in_lane = lanes >= lane
    in_row = lax.broadcasted_iota(jnp.int32, (8, 128), 0) >= row

    def wide(mask, rows):
        return jnp.concatenate([mask] * (rows // 8), axis=0) if rows > 8 else mask

    def tiles(part, offset, rows):
        start = pl.multiple_of(base_row + offset, 8)
        block = ext[part, pl.ds(start, rows), pl.ds(base_col, side + 128)]
        return jnp.where(wide(in_lane, rows), block[:, :128], block[:, side:]), block[:, 128:side]

    def window(part, offset, rows):
        near, far = tiles(part, offset, rows)
        if offset == 0:
            near_end, far_end = tiles(part, side, 8)
            near = jnp.concatenate([jnp.where(in_row, near[:8], near_end), near[8:]], axis=0)
            far = jnp.concatenate([jnp.where(in_row, far[:8], far_end), far[8:]], axis=0)
        out = jnp.concatenate([near, far], axis=1)
        view[part, offset:offset + rows] = out
        return out

    def put(high, low, which, rows, value):
        top_part, rest = split(value)
        high[which, rows] = top_part
        low[which, rows] = rest

    for at in range(0, half, step):
        def wave(offset):
            here = slice(offset, offset + step)
            vr, vi = window(0, offset, step), window(1, offset, step)
            pr, pi = probe[0, here], probe[1, here]
            return pr * vr - pi * vi, pr * vi + pi * vr

        upper_r, upper_i = wave(at)
        lower_r, lower_i = wave(half + at)
        put(a_high, a_low, 0, slice(at, at + step), upper_r + lower_r)
        put(a_high, a_low, 0, slice(half + at, half + at + step), upper_i + lower_i)
        put(a_high, a_low, 1, slice(at, at + step), upper_r - lower_r)
        put(a_high, a_low, 1, slice(half + at, half + at + step), upper_i - lower_i)

    def left_product(table, odd):
        fine, rough = table[odd, 1], table[odd, 0]
        return dot(jnp.concatenate([rough, rough, fine], axis=1),
                   jnp.concatenate([a_high[odd], a_low[odd], a_high[odd]], axis=0))

    def right_product(table, odd):
        fine, rough = table[odd, 1], table[odd, 0]
        return dot(jnp.concatenate([x_high[odd], x_low[odd], x_high[odd]], axis=1),
                   jnp.concatenate([rough, rough, fine], axis=0))

    for odd in (0, 1):
        out = left_product(left_table, odd)
        for at in range(0, half, step):
            real, imag = out[at:at + step], out[half + at:half + at + step]
            rows = slice(odd * half + at, odd * half + at + step)
            put(x_high, x_low, 0, rows, jnp.concatenate([real[:, :half] + real[:, half:], imag[:, :half] + imag[:, half:]], axis=1))
            put(x_high, x_low, 1, rows, jnp.concatenate([real[:, :half] - real[:, half:], imag[:, :half] - imag[:, half:]], axis=1))
    for odd in (0, 1):
        far = right_product(right_table, odd)
        for at in range(0, side, step):
            rows = slice(at, at + step)
            real, imag = far[rows, :half], far[rows, half:]
            keep = 1.0 - amp[odd, rows] * lax.rsqrt(jnp.maximum(real * real + imag * imag, 0.25))
            put(x_high, x_low, odd, rows, jnp.concatenate([real * keep, imag * keep], axis=1))
    even, odd_part = right_product(left_table, 0), right_product(left_table, 1)
    for at in range(0, side, step):
        rows = slice(at, at + step)
        total, difference = even[rows] + odd_part[rows], even[rows] - odd_part[rows]
        which, place = at // half, at % half
        put(a_high, a_low, which, slice(place, place + step), jnp.concatenate([total[:, :half], difference[:, :half]], axis=1))
        put(a_high, a_low, which, slice(half + place, half + place + step), jnp.concatenate([total[:, half:], difference[:, half:]], axis=1))
    even, odd_part = left_product(right_table, 0), left_product(right_table, 1)

    def add(part, offset, term):
        rows = term.shape[0]
        start = pl.multiple_of(base_row + offset, 8)
        here = wide(in_lane, rows)
        zero = jnp.zeros((rows, 128), F32)
        near, far = term[:, :128], term[:, 128:]
        grad[part, pl.ds(start, rows), pl.ds(base_col, side + 128)] += jnp.concatenate(
            [jnp.where(here, near, zero), far, jnp.where(here, zero, near)], axis=1)

    zero_row = jnp.zeros((8, side), F32)
    both_in_row = jnp.concatenate([in_row] * (side // 128), axis=1)
    for at in range(0, side, step):
        rows = slice(at, at + step)
        place = at % half
        if at < half:
            cr = even[place:place + step] + odd_part[place:place + step]
            ci = even[half + place:half + place + step] + odd_part[half + place:half + place + step]
        else:
            cr = even[place:place + step] - odd_part[place:place + step]
            ci = even[half + place:half + place + step] - odd_part[half + place:half + place + step]
        pr, pi = probe[0, rows], probe[1, rows]
        vr, vi = view[0, rows], view[1, rows]
        for part, term in enumerate((pr * cr + pi * ci, pr * ci - pi * cr)):
            if at == 0:
                add(part, side, jnp.where(both_in_row, zero_row, term[:8]))
                term = jnp.concatenate([jnp.where(both_in_row, term[:8], zero_row), term[8:]], axis=0)
            add(part, at, term)
        view[0, rows] = unrolled(vr * cr + vi * ci, lane, 1)
        view[1, rows] = unrolled(vr * ci - vi * cr, lane, 1)
    back = lax.rem(8 - row, 8)
    inside = lax.broadcasted_iota(jnp.int32, (8, side), 0) < 8 - row
    for part in (0, 1):
        opening = pltpu.roll(view[part, 0:8], back, 0)
        now = opening
        for at in range(0, side, 8):
            after = opening if at + 8 == side else pltpu.roll(view[part, at + 8:at + 16], back, 0)
            probe_acc[part, at:at + 8] += jnp.where(inside, now, after)
            now = after


def patches_kernel(off, tile, upper, lower, bottom, corner, probe, amp, left_table, right_table,
                   main_out, upper_out, lower_out, bottom_out, corner_out, probe_out, ext, grad, *scratch):
    side = upper.shape[2]
    rows, cols = tile.shape[1], tile.shape[2]
    ext[:, :rows, :cols] = tile[...]
    ext[:, :side, cols:] = upper[...]
    ext[:, side:rows, cols:] = lower[...]
    ext[:, rows:, :cols] = bottom[...]
    ext[:, rows:, cols:] = corner[...]
    grad[...] = jnp.zeros_like(grad)
    probe_out[...] = jnp.zeros_like(probe_out)

    def step(number, carry):
        one_patch(off[number, 0], off[number, 1], amp.at[number], probe.at[number], left_table, right_table,
                  ext, grad, probe_out, *scratch)
        return carry

    lax.fori_loop(0, amp.shape[0], step, 0)
    main_out[...] = grad[:, :rows, :cols]
    upper_out[...] = grad[:, :side, cols:]
    lower_out[...] = grad[:, side:rows, cols:]
    bottom_out[...] = grad[:, rows:, :cols]
    corner_out[...] = grad[:, rows:, cols:]


def all_patches(off, tile, upper, lower, bottom, corner, probe, amp):
    side = upper.shape[2]
    rows, cols = tile.shape[1], tile.shape[2]
    table = half_tables(side)
    tables = [jnp.asarray(split_table(table)), jnp.asarray(split_table(table.transpose(0, 2, 1)))]
    amps, probes = prepare(off, amp, probe)
    vmem = pl.BlockSpec(memory_space=pltpu.VMEM)
    shape = lambda *dims: jax.ShapeDtypeStruct(dims, F32)
    return pl.pallas_call(
        patches_kernel,
        out_shape=(shape(2, rows, cols), shape(2, side, side), shape(2, rows - side, side), shape(2, side, cols),
                   shape(2, side, side), shape(2, side, side)),
        in_specs=[pl.BlockSpec(memory_space=pltpu.SMEM)] + [vmem] * 9,
        out_specs=[vmem] * 6,
        scratch_shapes=[pltpu.VMEM((2, rows + side, cols + side), F32)] * 2
                     + [pltpu.VMEM((2, side, side), F32)] + [pltpu.VMEM((2, side, side), BF16)] * 4,
        compiler_params=pltpu.CompilerParams(vmem_limit_bytes=36 * 1024 * 1024),
    )(off, tile, upper, lower, bottom, corner, probes, amps, *tables)


ACROSS, LINES = (2, 4, 6), (4, 8, 12)


def exchanged(pieces, distances, axis):
    return [lax.ppermute(piece, axis, [(i, i ^ distance) for i in range(lax.axis_size(axis))])
            for piece, distance in zip(pieces, distances)]


def added(parts):
    while len(parts) > 1:
        parts = [parts[i] + parts[i + 1] for i in range(0, len(parts), 2)]
    return parts[0]


def scattered(value, me, distances, axis):
    rows = value.shape[0] // 4
    pieces = [lax.dynamic_slice_in_dim(value, (me ^ place) * rows, rows, 0) for place in range(4)]
    return added(pieces[:1] + exchanged(pieces[1:], distances, axis))


def everywhere(value, distances, axis):
    return added([value] + exchanged([value] * 3, distances, axis))


def gathered(value, me, distances, axis):
    rows = value.shape[0]
    whole = jnp.zeros((rows * 4, value.shape[1]), value.dtype)
    for place, part in enumerate([value] + exchanged([value] * 3, distances, axis)):
        whole = lax.dynamic_update_slice_in_dim(whole, part, (me ^ place) * rows, 0)
    return whole


def summed_everywhere(value):
    shape = value.shape
    value = value.reshape(-1, shape[-1])
    chip = (lax.axis_index("row") >> 1) & 3
    line = lax.axis_index("col") >> 2
    value = scattered(value, chip, ACROSS, "row")
    value = scattered(value, line, LINES, "col")
    value = everywhere(value, (1, 8, 9), "row")
    value = everywhere(value, (1, 2, 3), "col")
    value = gathered(value, line, LINES, "col")
    value = gathered(value, chip, ACROSS, "row")
    return value.reshape(shape)


def shards_body(object_field, probe, amplitude, offsets):
    side = probe.shape[1]
    upper = passed_along(object_field[:, :side, :side], "col", -1)
    lower = passed_along(object_field[:, side:, :side], "col", -1)
    bottom = passed_along(object_field[:, :side, :], "row", -1)
    corner = passed_along(upper, "row", -1)
    main, upper, lower, bottom, corner, probe_acc = all_patches(
        offsets[0, 0], object_field, upper, lower, bottom, corner, probe, amplitude[0, 0])
    corner_back = passed_along(corner, "row", 1)
    lower_back = passed_along(lower, "col", 1)
    bottom_back = passed_along(bottom, "row", 1)
    upper_back = passed_along(upper + corner_back, "col", 1)
    count = amplitude.shape[2] * lax.axis_size("row") * lax.axis_size("col")
    probe_total = summed_everywhere(probe_acc) / count
    right_back = jnp.concatenate([upper_back, lower_back], axis=1)
    main = main.at[:, :side, :].add(bottom_back)
    object_grad = main.at[:, :, :side].add(right_back)
    return (object_grad, probe_total)


def solution(mesh):
    placed = (
        P(None, "row", "col"),
        P(),
        P("row", "col", None, None, None),
        P("row", "col", None, None),
    )
    return jax.shard_map(
        shards_body, mesh=mesh, in_specs=placed, out_specs=(P(None, "row", "col"), P()), check_vma=False
    )
```

```python
import functools
import math

import jax
import jax.numpy as jnp
import numpy as np
from jax import lax
from jax.experimental import pallas as pl
from jax.experimental.pallas import tpu as pltpu
from jax.sharding import PartitionSpec as P


F32 = jnp.float32
BF16 = jnp.bfloat16


def passed_along(value, axis, steps):
    count = lax.axis_size(axis)
    first, last = (max(0, -steps), min(count, count - steps))
    return lax.ppermute(value, axis, [(source, source + steps) for source in range(first, last)])


def split(value):
    high = value.astype(BF16)
    return high, (value - high.astype(F32)).astype(BF16)


def half_tables(size):
    half = size // 2
    tables = []
    for odd in (0, 1):
        angle = ((2 * np.arange(half)[:, None] + odd) * np.arange(half)[None, :] % size) * (2.0 * math.pi / size)
        cosine, sine = np.cos(angle) / math.sqrt(size), np.sin(angle) / math.sqrt(size)
        tables.append(np.block([[cosine, sine], [-sine, cosine]]).astype(np.float32))
    return np.stack(tables)


def split_table(table):
    high = table.astype(BF16)
    return np.stack([high, (table - high.astype(np.float32)).astype(BF16)], axis=1)


def dot(left, right):
    return jnp.dot(left, right, preferred_element_type=F32)


def rolled(block, shift, axis):
    size = block.shape[axis]
    small = 8 if axis == 0 else 128
    count = size // small
    pieces = []
    for index in range(count):
        piece = block[index * small:(index + 1) * small] if axis == 0 else block[:, index * small:(index + 1) * small]
        pieces.append(pltpu.roll(piece, shift, axis))
    place = lax.broadcasted_iota(jnp.int32, pieces[0].shape, axis)
    inside = place >= shift
    out = [jnp.where(inside, pieces[index], pieces[index - 1]) for index in range(count)]
    return jnp.concatenate(out, axis=axis)


def unrolled(block, shift, axis):
    size = block.shape[axis]
    small = 8 if axis == 0 else 128
    count = size // small
    back = lax.rem(small - shift, small)
    pieces = []
    for index in range(count):
        piece = block[index * small:(index + 1) * small] if axis == 0 else block[:, index * small:(index + 1) * small]
        pieces.append(pltpu.roll(piece, back, axis))
    place = lax.broadcasted_iota(jnp.int32, pieces[0].shape, axis)
    inside = place < small - shift
    out = [jnp.where(inside, pieces[index], pieces[(index + 1) % count]) for index in range(count)]
    return jnp.concatenate(out, axis=axis)


def prepare_kernel(off, amp, probe, pick, amp_out, probe_out):
    number = pl.program_id(0)
    side = probe.shape[1]
    half = side // 2
    row, lane = lax.rem(off[number, 0], 8), lax.rem(off[number, 1], 128)
    high, low = split(amp[0])
    high, low = split(dot(high, pick[0]) + dot(low, pick[0]))
    both = dot(pick[1], high) + dot(pick[1], low)
    amp_out[0, 0] = both[:, :half]
    amp_out[0, 1] = both[:, half:]
    for part in (0, 1):
        probe_out[0, part] = rolled(rolled(probe[part], row, 0), lane, 1)


def prepare(off, amp, probe):
    count, side = amp.shape[0], amp.shape[1]
    half = side // 2
    pick = np.zeros((side, side), np.float32)
    pick[2 * np.arange(half), np.arange(half)] = 1.0
    pick[2 * np.arange(half) + 1, half + np.arange(half)] = 1.0
    return pl.pallas_call(
        prepare_kernel,
        grid=(count,),
        out_shape=(jax.ShapeDtypeStruct((count, 2, side, half), F32), jax.ShapeDtypeStruct((count, 2, side, side), F32)),
        in_specs=[pl.BlockSpec(memory_space=pltpu.SMEM),
                  pl.BlockSpec((1, side, side), lambda i: (i, 0, 0)),
                  pl.BlockSpec((2, side, side), lambda i: (0, 0, 0)),
                  pl.BlockSpec((2, side, side), lambda i: (0, 0, 0))],
        out_specs=(pl.BlockSpec((1, 2, side, half), lambda i: (i, 0, 0, 0)),
                   pl.BlockSpec((1, 2, side, side), lambda i: (i, 0, 0, 0))),
    )(off, amp, probe, jnp.asarray(np.stack([pick, pick.T]).astype(BF16)))


def one_patch(top, left, amp, probe, left_table, right_table, ext, grad, probe_acc,
              view, a_high, a_low, x_high, x_low):
    side = probe.shape[1]
    half, step = side // 2, 32
    base_row = pl.multiple_of(top // 8 * 8, 8)
    base_col = pl.multiple_of(left // 128 * 128, 128)
    row, lane = top - base_row, left - base_col
    lanes = lax.broadcasted_iota(jnp.int32, (8, 128), 1)
    in_lane = lanes >= lane
    in_row = lax.broadcasted_iota(jnp.int32, (8, 128), 0) >= row

    def wide(mask, rows):
        return jnp.concatenate([mask] * (rows // 8), axis=0) if rows > 8 else mask

    def tiles(part, offset, rows):
        start = pl.multiple_of(base_row + offset, 8)
        block = ext[part, pl.ds(start, rows), pl.ds(base_col, side + 128)]
        return jnp.where(wide(in_lane, rows), block[:, :128], block[:, side:]), block[:, 128:side]

    def window(part, offset, rows):
        near, far = tiles(part, offset, rows)
        if offset == 0:
            near_end, far_end = tiles(part, side, 8)
            near = jnp.concatenate([jnp.where(in_row, near[:8], near_end), near[8:]], axis=0)
            far = jnp.concatenate([jnp.where(in_row, far[:8], far_end), far[8:]], axis=0)
        out = jnp.concatenate([near, far], axis=1)
        view[part, offset:offset + rows] = out
        return out

    def put(high, low, which, rows, value):
        top_part, rest = split(value)
        high[which, rows] = top_part
        low[which, rows] = rest

    for at in range(0, half, step):
        def wave(offset):
            here = slice(offset, offset + step)
            vr, vi = window(0, offset, step), window(1, offset, step)
            pr, pi = probe[0, here], probe[1, here]
            return pr * vr - pi * vi, pr * vi + pi * vr

        upper_r, upper_i = wave(at)
        lower_r, lower_i = wave(half + at)
        put(a_high, a_low, 0, slice(at, at + step), upper_r + lower_r)
        put(a_high, a_low, 0, slice(half + at, half + at + step), upper_i + lower_i)
        put(a_high, a_low, 1, slice(at, at + step), upper_r - lower_r)
        put(a_high, a_low, 1, slice(half + at, half + at + step), upper_i - lower_i)

    def left_product(table, odd):
        fine, rough = table[odd, 1], table[odd, 0]
        return dot(jnp.concatenate([rough, rough, fine], axis=1),
                   jnp.concatenate([a_high[odd], a_low[odd], a_high[odd]], axis=0))

    def right_product(table, odd):
        fine, rough = table[odd, 1], table[odd, 0]
        return dot(jnp.concatenate([x_high[odd], x_low[odd], x_high[odd]], axis=1),
                   jnp.concatenate([rough, rough, fine], axis=0))

    for odd in (0, 1):
        out = left_product(left_table, odd)
        for at in range(0, half, step):
            real, imag = out[at:at + step], out[half + at:half + at + step]
            rows = slice(odd * half + at, odd * half + at + step)
            put(x_high, x_low, 0, rows, jnp.concatenate([real[:, :half] + real[:, half:], imag[:, :half] + imag[:, half:]], axis=1))
            put(x_high, x_low, 1, rows, jnp.concatenate([real[:, :half] - real[:, half:], imag[:, :half] - imag[:, half:]], axis=1))
    for odd in (0, 1):
        far = right_product(right_table, odd)
        for at in range(0, side, step):
            rows = slice(at, at + step)
            real, imag = far[rows, :half], far[rows, half:]
            keep = 1.0 - amp[odd, rows] * lax.rsqrt(jnp.maximum(real * real + imag * imag, 0.25))
            put(x_high, x_low, odd, rows, jnp.concatenate([real * keep, imag * keep], axis=1))
    even, odd_part = right_product(left_table, 0), right_product(left_table, 1)
    for at in range(0, side, step):
        rows = slice(at, at + step)
        total, difference = even[rows] + odd_part[rows], even[rows] - odd_part[rows]
        which, place = at // half, at % half
        put(a_high, a_low, which, slice(place, place + step), jnp.concatenate([total[:, :half], difference[:, :half]], axis=1))
        put(a_high, a_low, which, slice(half + place, half + place + step), jnp.concatenate([total[:, half:], difference[:, half:]], axis=1))
    even, odd_part = left_product(right_table, 0), left_product(right_table, 1)

    def add(part, offset, term):
        rows = term.shape[0]
        start = pl.multiple_of(base_row + offset, 8)
        here = wide(in_lane, rows)
        zero = jnp.zeros((rows, 128), F32)
        near, far = term[:, :128], term[:, 128:]
        grad[part, pl.ds(start, rows), pl.ds(base_col, side + 128)] += jnp.concatenate(
            [jnp.where(here, near, zero), far, jnp.where(here, zero, near)], axis=1)

    zero_row = jnp.zeros((8, side), F32)
    both_in_row = jnp.concatenate([in_row] * (side // 128), axis=1)
    for at in range(0, side, step):
        rows = slice(at, at + step)
        place = at % half
        if at < half:
            cr = even[place:place + step] + odd_part[place:place + step]
            ci = even[half + place:half + place + step] + odd_part[half + place:half + place + step]
        else:
            cr = even[place:place + step] - odd_part[place:place + step]
            ci = even[half + place:half + place + step] - odd_part[half + place:half + place + step]
        pr, pi = probe[0, rows], probe[1, rows]
        vr, vi = view[0, rows], view[1, rows]
        for part, term in enumerate((pr * cr + pi * ci, pr * ci - pi * cr)):
            if at == 0:
                add(part, side, jnp.where(both_in_row, zero_row, term[:8]))
                term = jnp.concatenate([jnp.where(both_in_row, term[:8], zero_row), term[8:]], axis=0)
            add(part, at, term)
        view[0, rows] = unrolled(vr * cr + vi * ci, lane, 1)
        view[1, rows] = unrolled(vr * ci - vi * cr, lane, 1)
    back = lax.rem(8 - row, 8)
    inside = lax.broadcasted_iota(jnp.int32, (8, side), 0) < 8 - row
    for part in (0, 1):
        opening = pltpu.roll(view[part, 0:8], back, 0)
        now = opening
        for at in range(0, side, 8):
            after = opening if at + 8 == side else pltpu.roll(view[part, at + 8:at + 16], back, 0)
            probe_acc[part, at:at + 8] += jnp.where(inside, now, after)
            now = after


def patches_kernel(off, tile, upper, middle, lower, bottom, corner, probe, amp, left_table, right_table,
                   main_out, upper_out, lower_out, bottom_out, corner_out, probe_out, ext, grad, *scratch, scale):
    side = upper.shape[2]
    rows, cols = tile.shape[1], tile.shape[2]
    cut = rows - lower.shape[1]
    number = pl.program_id(0)

    @pl.when(number == 0)
    def opening():
        ext[:, :rows, :cols] = tile[...]
        ext[:, :side, cols:] = upper[...]
        ext[:, side:cut, cols:] = middle[...]
        ext[:, cut:rows, cols:] = lower[...]
        ext[:, rows:, :cols] = bottom[...]
        ext[:, rows:, cols:] = corner[...]
        grad[...] = jnp.zeros_like(grad)
        probe_out[...] = jnp.zeros_like(probe_out)

    one_patch(off[number, 0], off[number, 1], amp.at[0], probe.at[0], left_table, right_table,
              ext, grad, probe_out, *scratch)

    @pl.when(number == pl.num_programs(0) - 1)
    def closing():
        main_out[...] = grad[:, :rows, :cols]
        upper_out[...] = grad[:, :side, cols:]
        lower_out[...] = grad[:, side:rows, cols:]
        bottom_out[...] = grad[:, rows:, :cols]
        corner_out[...] = grad[:, rows:, cols:]
        probe_out[...] *= scale


def all_patches(off, tile, upper, middle, lower, bottom, corner, probe, amp, scale):
    count, side = amp.shape[0], upper.shape[2]
    rows, cols = tile.shape[1], tile.shape[2]
    table = half_tables(side)
    tables = [jnp.asarray(split_table(table)), jnp.asarray(split_table(table.transpose(0, 2, 1)))]
    amps, probes = prepare(off, amp, probe)
    vmem = pl.BlockSpec(memory_space=pltpu.VMEM)
    shape = lambda *dims: jax.ShapeDtypeStruct(dims, F32)
    return pl.pallas_call(
        functools.partial(patches_kernel, scale=scale),
        grid=(count,),
        out_shape=(shape(2, rows, cols), shape(2, side, side), shape(2, rows - side, side), shape(2, side, cols),
                   shape(2, side, side), shape(2, side, side)),
        in_specs=[pl.BlockSpec(memory_space=pltpu.SMEM)] + [vmem] * 6
                 + [pl.BlockSpec((1, 2, side, side), lambda i: (i, 0, 0, 0)),
                    pl.BlockSpec((1, 2, side, side // 2), lambda i: (i, 0, 0, 0))] + [vmem] * 2,
        out_specs=[vmem] * 6,
        scratch_shapes=[pltpu.VMEM((2, rows + side, cols + side), F32)] * 2
                     + [pltpu.VMEM((2, side, side), F32)] + [pltpu.VMEM((2, side, side), BF16)] * 4,
        compiler_params=pltpu.CompilerParams(vmem_limit_bytes=50 * 1024 * 1024),
    )(off, tile, upper, middle, lower, bottom, corner, probes, amps, *tables)


ACROSS, LINES = (2, 4, 6), (4, 8, 12)


def exchanged(pieces, distances, axis):
    return [lax.ppermute(piece, axis, [(i, i ^ distance) for i in range(lax.axis_size(axis))])
            for piece, distance in zip(pieces, distances)]


def added(parts):
    while len(parts) > 1:
        parts = [parts[i] + parts[i + 1] for i in range(0, len(parts), 2)]
    return parts[0]


def scattered(value, me, distances, axis):
    rows = value.shape[0] // 4
    pieces = [lax.dynamic_slice_in_dim(value, (me ^ place) * rows, rows, 0) for place in range(4)]
    return added(pieces[:1] + exchanged(pieces[1:], distances, axis))


def everywhere(value, distances, axis):
    return added([value] + exchanged([value] * 3, distances, axis))


def gathered(value, me, distances, axis):
    rows = value.shape[0]
    whole = jnp.zeros((rows * 4, value.shape[1]), value.dtype)
    for place, part in enumerate([value] + exchanged([value] * 3, distances, axis)):
        whole = lax.dynamic_update_slice_in_dim(whole, part, (me ^ place) * rows, 0)
    return whole


def halved(value, distance, axis):
    rows = value.shape[0] // 2
    upper = (lax.axis_index(axis) & distance) != 0
    low, high = value[:rows], value[rows:]
    got, = exchanged([jnp.where(upper, low, high)], (distance,), axis)
    return jnp.where(upper, high, low) + got


def doubled(value, distance, axis):
    upper = (lax.axis_index(axis) & distance) != 0
    got, = exchanged([value], (distance,), axis)
    return jnp.concatenate([jnp.where(upper, got, value), jnp.where(upper, value, got)], axis=0)


def round_ring(value, step):
    size = lax.axis_size("col")
    return lax.ppermute(value, "col", [(i, i // 4 * 4 + (i + step) % 4) for i in range(size)])


def ring_sum(value):
    held = [value]
    for _ in range(3):
        held.append(round_ring(held[-1], -1))
    return (held[0] + held[2]) + (held[1] + held[3])


def summed_everywhere(value):
    shape = value.shape
    value = value.reshape(-1, shape[-1])
    chip = (lax.axis_index("row") >> 1) & 3
    value = halved(value, 1, "row")
    value = scattered(value, chip, ACROSS, "row")
    value = everywhere(value, LINES, "col")
    value = value + exchanged([value], (8,), "row")[0]
    value = ring_sum(value)
    value = gathered(value, chip, ACROSS, "row")
    value = doubled(value, 1, "row")
    return value.reshape(shape)


def long_way(value):
    value = round_ring(value, 1)
    value = round_ring(value, 1)
    pairs = []
    for source in range(lax.axis_size("col")):
        line, place = source // 4, source % 4
        if place != 2:
            pairs.append((source, line * 4 + (place + 1) % 4))
        elif line > 0:
            pairs.append((source, line * 4 - 1))
    return lax.ppermute(value, "col", pairs)


def shards_body(object_field, probe, amplitude, offsets):
    side = probe.shape[1]
    cut = object_field.shape[1] - side // 2
    lower = long_way(object_field[:, cut:, :side])
    upper = passed_along(object_field[:, :side, :side], "col", -1)
    middle = passed_along(object_field[:, side:cut, :side], "col", -1)
    bottom = passed_along(object_field[:, :side, :], "row", -1)
    corner = passed_along(upper, "row", -1)
    count = amplitude.shape[2] * lax.axis_size("row") * lax.axis_size("col")
    main, upper, lower, bottom, corner, probe_acc = all_patches(
        offsets[0, 0], object_field, upper, middle, lower, bottom, corner, probe, amplitude[0, 0], 1.0 / count)
    corner_back = passed_along(corner, "row", 1)
    lower_back = passed_along(lower, "col", 1)
    bottom_back = passed_along(bottom, "row", 1)
    upper_back = passed_along(upper + corner_back, "col", 1)
    probe_total = summed_everywhere(probe_acc)
    right_back = jnp.concatenate([upper_back, lower_back], axis=1)
    main = main.at[:, :side, :].add(bottom_back)
    object_grad = main.at[:, :, :side].add(right_back)
    return (object_grad, probe_total)


def solution(mesh):
    placed = (
        P(None, "row", "col"),
        P(),
        P("row", "col", None, None, None),
        P("row", "col", None, None),
    )
    return jax.shard_map(
        shards_body, mesh=mesh, in_specs=placed, out_specs=(P(None, "row", "col"), P()), check_vma=False
    )
```

```python
import functools
import math

import jax
import jax.numpy as jnp
import numpy as np
from jax import lax
from jax.experimental import pallas as pl
from jax.experimental.pallas import tpu as pltpu
from jax.sharding import PartitionSpec as P


F32 = jnp.float32
BF16 = jnp.bfloat16


def passed_along(value, axis, steps):
    count = lax.axis_size(axis)
    first, last = (max(0, -steps), min(count, count - steps))
    return lax.ppermute(value, axis, [(source, source + steps) for source in range(first, last)])


def split(value):
    high = value.astype(BF16)
    return high, (value - high.astype(F32)).astype(BF16)


def half_tables(size):
    half = size // 2
    tables = []
    for odd in (0, 1):
        angle = ((2 * np.arange(half)[:, None] + odd) * np.arange(half)[None, :] % size) * (2.0 * math.pi / size)
        cosine, sine = np.cos(angle) / math.sqrt(size), np.sin(angle) / math.sqrt(size)
        tables.append(np.block([[cosine, sine], [-sine, cosine]]).astype(np.float32))
    return np.stack(tables)


def split_table(table):
    high = table.astype(BF16)
    return np.stack([high, (table - high.astype(np.float32)).astype(BF16)], axis=1)


def dot(left, right):
    return jnp.dot(left, right, preferred_element_type=F32)


def rolled(block, shift, axis):
    size = block.shape[axis]
    small = 8 if axis == 0 else 128
    count = size // small
    pieces = []
    for index in range(count):
        piece = block[index * small:(index + 1) * small] if axis == 0 else block[:, index * small:(index + 1) * small]
        pieces.append(pltpu.roll(piece, shift, axis))
    place = lax.broadcasted_iota(jnp.int32, pieces[0].shape, axis)
    inside = place >= shift
    out = [jnp.where(inside, pieces[index], pieces[index - 1]) for index in range(count)]
    return jnp.concatenate(out, axis=axis)


def unrolled(block, shift, axis):
    size = block.shape[axis]
    small = 8 if axis == 0 else 128
    count = size // small
    back = lax.rem(small - shift, small)
    pieces = []
    for index in range(count):
        piece = block[index * small:(index + 1) * small] if axis == 0 else block[:, index * small:(index + 1) * small]
        pieces.append(pltpu.roll(piece, back, axis))
    place = lax.broadcasted_iota(jnp.int32, pieces[0].shape, axis)
    inside = place < small - shift
    out = [jnp.where(inside, pieces[index], pieces[(index + 1) % count]) for index in range(count)]
    return jnp.concatenate(out, axis=axis)


def prepare_kernel(off, amp, probe, pick, amp_out, probe_out):
    number = pl.program_id(0)
    side = probe.shape[1]
    half = side // 2
    row, lane = lax.rem(off[number, 0], 8), lax.rem(off[number, 1], 128)
    high, low = split(amp[0])
    high, low = split(dot(high, pick[0]) + dot(low, pick[0]))
    both = dot(pick[1], high) + dot(pick[1], low)
    amp_out[0, 0] = both[:, :half]
    amp_out[0, 1] = both[:, half:]
    for part in (0, 1):
        probe_out[0, part] = rolled(rolled(probe[part], row, 0), lane, 1)


def prepare(off, amp, probe):
    count, side = amp.shape[0], amp.shape[1]
    half = side // 2
    pick = np.zeros((side, side), np.float32)
    pick[2 * np.arange(half), np.arange(half)] = 1.0
    pick[2 * np.arange(half) + 1, half + np.arange(half)] = 1.0
    return pl.pallas_call(
        prepare_kernel,
        grid=(count,),
        out_shape=(jax.ShapeDtypeStruct((count, 2, side, half), F32), jax.ShapeDtypeStruct((count, 2, side, side), F32)),
        in_specs=[pl.BlockSpec(memory_space=pltpu.SMEM),
                  pl.BlockSpec((1, side, side), lambda i: (i, 0, 0)),
                  pl.BlockSpec((2, side, side), lambda i: (0, 0, 0)),
                  pl.BlockSpec((2, side, side), lambda i: (0, 0, 0))],
        out_specs=(pl.BlockSpec((1, 2, side, half), lambda i: (i, 0, 0, 0)),
                   pl.BlockSpec((1, 2, side, side), lambda i: (i, 0, 0, 0))),
    )(off, amp, probe, jnp.asarray(np.stack([pick, pick.T]).astype(BF16)))


def one_patch(top, left, amp, probe, left_table, right_table, ext, grad, probe_acc,
              view, a_high, a_low, x_high, x_low):
    side = probe.shape[1]
    half, step = side // 2, 32
    base_row = pl.multiple_of(top // 8 * 8, 8)
    base_col = pl.multiple_of(left // 128 * 128, 128)
    row, lane = top - base_row, left - base_col
    lanes = lax.broadcasted_iota(jnp.int32, (8, 128), 1)
    in_lane = lanes >= lane
    in_row = lax.broadcasted_iota(jnp.int32, (8, 128), 0) >= row

    def wide(mask, rows):
        return jnp.concatenate([mask] * (rows // 8), axis=0) if rows > 8 else mask

    def tiles(part, offset, rows):
        start = pl.multiple_of(base_row + offset, 8)
        block = ext[part, pl.ds(start, rows), pl.ds(base_col, side + 128)]
        return jnp.where(wide(in_lane, rows), block[:, :128], block[:, side:]), block[:, 128:side]

    def window(part, offset, rows):
        near, far = tiles(part, offset, rows)
        if offset == 0:
            near_end, far_end = tiles(part, side, 8)
            near = jnp.concatenate([jnp.where(in_row, near[:8], near_end), near[8:]], axis=0)
            far = jnp.concatenate([jnp.where(in_row, far[:8], far_end), far[8:]], axis=0)
        out = jnp.concatenate([near, far], axis=1)
        view[part, offset:offset + rows] = out
        return out

    def put(high, low, which, rows, value):
        top_part, rest = split(value)
        high[which, rows] = top_part
        low[which, rows] = rest

    for at in range(0, half, step):
        def wave(offset):
            here = slice(offset, offset + step)
            vr, vi = window(0, offset, step), window(1, offset, step)
            pr, pi = probe[0, here], probe[1, here]
            return pr * vr - pi * vi, pr * vi + pi * vr

        upper_r, upper_i = wave(at)
        lower_r, lower_i = wave(half + at)
        put(a_high, a_low, 0, slice(at, at + step), upper_r + lower_r)
        put(a_high, a_low, 0, slice(half + at, half + at + step), upper_i + lower_i)
        put(a_high, a_low, 1, slice(at, at + step), upper_r - lower_r)
        put(a_high, a_low, 1, slice(half + at, half + at + step), upper_i - lower_i)

    yield

    def left_product(table, odd):
        fine, rough = table[odd, 1], table[odd, 0]
        return dot(jnp.concatenate([rough, rough, fine], axis=1),
                   jnp.concatenate([a_high[odd], a_low[odd], a_high[odd]], axis=0))

    def right_product(table, odd):
        fine, rough = table[odd, 1], table[odd, 0]
        return dot(jnp.concatenate([x_high[odd], x_low[odd], x_high[odd]], axis=1),
                   jnp.concatenate([rough, rough, fine], axis=0))

    for odd in (0, 1):
        out = left_product(left_table, odd)
        for at in range(0, half, step):
            real, imag = out[at:at + step], out[half + at:half + at + step]
            rows = slice(odd * half + at, odd * half + at + step)
            put(x_high, x_low, 0, rows, jnp.concatenate([real[:, :half] + real[:, half:], imag[:, :half] + imag[:, half:]], axis=1))
            put(x_high, x_low, 1, rows, jnp.concatenate([real[:, :half] - real[:, half:], imag[:, :half] - imag[:, half:]], axis=1))
    yield
    for odd in (0, 1):
        far = right_product(right_table, odd)
        for at in range(0, side, step):
            rows = slice(at, at + step)
            real, imag = far[rows, :half], far[rows, half:]
            keep = 1.0 - amp[odd, rows] * lax.rsqrt(jnp.maximum(real * real + imag * imag, 0.25))
            put(x_high, x_low, odd, rows, jnp.concatenate([real * keep, imag * keep], axis=1))
    yield
    even, odd_part = right_product(left_table, 0), right_product(left_table, 1)
    for at in range(0, side, step):
        rows = slice(at, at + step)
        total, difference = even[rows] + odd_part[rows], even[rows] - odd_part[rows]
        which, place = at // half, at % half
        put(a_high, a_low, which, slice(place, place + step), jnp.concatenate([total[:, :half], difference[:, :half]], axis=1))
        put(a_high, a_low, which, slice(half + place, half + place + step), jnp.concatenate([total[:, half:], difference[:, half:]], axis=1))
    yield
    even, odd_part = left_product(right_table, 0), left_product(right_table, 1)

    def add(part, offset, term):
        rows = term.shape[0]
        start = pl.multiple_of(base_row + offset, 8)
        here = wide(in_lane, rows)
        zero = jnp.zeros((rows, 128), F32)
        near, far = term[:, :128], term[:, 128:]
        grad[part, pl.ds(start, rows), pl.ds(base_col, side + 128)] += jnp.concatenate(
            [jnp.where(here, near, zero), far, jnp.where(here, zero, near)], axis=1)

    zero_row = jnp.zeros((8, side), F32)
    both_in_row = jnp.concatenate([in_row] * (side // 128), axis=1)
    for at in range(0, side, step):
        rows = slice(at, at + step)
        place = at % half
        if at < half:
            cr = even[place:place + step] + odd_part[place:place + step]
            ci = even[half + place:half + place + step] + odd_part[half + place:half + place + step]
        else:
            cr = even[place:place + step] - odd_part[place:place + step]
            ci = even[half + place:half + place + step] - odd_part[half + place:half + place + step]
        pr, pi = probe[0, rows], probe[1, rows]
        vr, vi = view[0, rows], view[1, rows]
        for part, term in enumerate((pr * cr + pi * ci, pr * ci - pi * cr)):
            if at == 0:
                add(part, side, jnp.where(both_in_row, zero_row, term[:8]))
                term = jnp.concatenate([jnp.where(both_in_row, term[:8], zero_row), term[8:]], axis=0)
            add(part, at, term)
        view[0, rows] = unrolled(vr * cr + vi * ci, lane, 1)
        view[1, rows] = unrolled(vr * ci - vi * cr, lane, 1)
    yield
    back = lax.rem(8 - row, 8)
    inside = lax.broadcasted_iota(jnp.int32, (8, side), 0) < 8 - row
    for part in (0, 1):
        opening = pltpu.roll(view[part, 0:8], back, 0)
        now = opening
        for at in range(0, side, 8):
            after = opening if at + 8 == side else pltpu.roll(view[part, at + 8:at + 16], back, 0)
            probe_acc[part, at:at + 8] += jnp.where(inside, now, after)
            now = after


def interleaved(patches):
    running = list(patches)
    while running:
        running = [patch for patch in running if next(patch, running) is None]


def patches_kernel(off, tile, upper, middle, lower, bottom, corner, probe, amp, left_table, right_table,
                   main_out, upper_out, lower_out, bottom_out, corner_out, probe_out, ext, grad, *scratch, scale):
    side = upper.shape[2]
    rows, cols = tile.shape[1], tile.shape[2]
    cut = rows - lower.shape[1]
    number = pl.program_id(0)

    @pl.when(number == 0)
    def opening():
        ext[:, :rows, :cols] = tile[...]
        ext[:, :side, cols:] = upper[...]
        ext[:, side:cut, cols:] = middle[...]
        ext[:, cut:rows, cols:] = lower[...]
        ext[:, rows:, :cols] = bottom[...]
        ext[:, rows:, cols:] = corner[...]
        grad[...] = jnp.zeros_like(grad)
        probe_out[...] = jnp.zeros_like(probe_out)

    together = amp.shape[0]
    interleaved(
        one_patch(off[number * together + which, 0], off[number * together + which, 1], amp.at[which], probe.at[which],
                  left_table, right_table, ext, grad, probe_out, *[ref.at[which] for ref in scratch])
        for which in range(together))

    @pl.when(number == pl.num_programs(0) - 1)
    def closing():
        main_out[...] = grad[:, :rows, :cols]
        upper_out[...] = grad[:, :side, cols:]
        lower_out[...] = grad[:, side:rows, cols:]
        bottom_out[...] = grad[:, rows:, :cols]
        corner_out[...] = grad[:, rows:, cols:]
        probe_out[...] *= scale


def all_patches(off, tile, upper, middle, lower, bottom, corner, probe, amp, scale):
    count, side = amp.shape[0], upper.shape[2]
    together = 2 if count % 2 == 0 else 1
    rows, cols = tile.shape[1], tile.shape[2]
    table = half_tables(side)
    tables = [jnp.asarray(split_table(table)), jnp.asarray(split_table(table.transpose(0, 2, 1)))]
    amps, probes = prepare(off, amp, probe)
    vmem = pl.BlockSpec(memory_space=pltpu.VMEM)
    shape = lambda *dims: jax.ShapeDtypeStruct(dims, F32)
    return pl.pallas_call(
        functools.partial(patches_kernel, scale=scale),
        grid=(count // together,),
        out_shape=(shape(2, rows, cols), shape(2, side, side), shape(2, rows - side, side), shape(2, side, cols),
                   shape(2, side, side), shape(2, side, side)),
        in_specs=[pl.BlockSpec(memory_space=pltpu.SMEM)] + [vmem] * 6
                 + [pl.BlockSpec((together, 2, side, side), lambda i: (i, 0, 0, 0)),
                    pl.BlockSpec((together, 2, side, side // 2), lambda i: (i, 0, 0, 0))] + [vmem] * 2,
        out_specs=[vmem] * 6,
        scratch_shapes=[pltpu.VMEM((2, rows + side, cols + side), F32)] * 2
                     + [pltpu.VMEM((together, 2, side, side), F32)] + [pltpu.VMEM((together, 2, side, side), BF16)] * 4,
        compiler_params=pltpu.CompilerParams(vmem_limit_bytes=50 * 1024 * 1024),
    )(off, tile, upper, middle, lower, bottom, corner, probes, amps, *tables)


ACROSS, LINES = (2, 4, 6), (4, 8, 12)


def exchanged(pieces, distances, axis):
    return [lax.ppermute(piece, axis, [(i, i ^ distance) for i in range(lax.axis_size(axis))])
            for piece, distance in zip(pieces, distances)]


def added(parts):
    while len(parts) > 1:
        parts = [parts[i] + parts[i + 1] for i in range(0, len(parts), 2)]
    return parts[0]


def scattered(value, me, distances, axis):
    rows = value.shape[0] // 4
    pieces = [lax.dynamic_slice_in_dim(value, (me ^ place) * rows, rows, 0) for place in range(4)]
    return added(pieces[:1] + exchanged(pieces[1:], distances, axis))


def everywhere(value, distances, axis):
    return added([value] + exchanged([value] * 3, distances, axis))


def gathered(value, me, distances, axis):
    rows = value.shape[0]
    whole = jnp.zeros((rows * 4, value.shape[1]), value.dtype)
    for place, part in enumerate([value] + exchanged([value] * 3, distances, axis)):
        whole = lax.dynamic_update_slice_in_dim(whole, part, (me ^ place) * rows, 0)
    return whole


def halved(value, distance, axis):
    rows = value.shape[0] // 2
    upper = (lax.axis_index(axis) & distance) != 0
    low, high = value[:rows], value[rows:]
    got, = exchanged([jnp.where(upper, low, high)], (distance,), axis)
    return jnp.where(upper, high, low) + got


def doubled(value, distance, axis):
    upper = (lax.axis_index(axis) & distance) != 0
    got, = exchanged([value], (distance,), axis)
    return jnp.concatenate([jnp.where(upper, got, value), jnp.where(upper, value, got)], axis=0)


def round_ring(value, step):
    size = lax.axis_size("col")
    return lax.ppermute(value, "col", [(i, i // 4 * 4 + (i + step) % 4) for i in range(size)])


def summed_everywhere(value):
    shape = value.shape
    value = value.reshape(-1, shape[-1])
    chip = (lax.axis_index("row") >> 1) & 3
    value = halved(value, 1, "row")
    value = scattered(value, chip, ACROSS, "row")
    value = everywhere(value, LINES, "col")
    value = value + exchanged([value], (8,), "row")[0]
    value = everywhere(value, (1, 2, 3), "col")
    value = gathered(value, chip, ACROSS, "row")
    value = doubled(value, 1, "row")
    return value.reshape(shape)


def long_way(value):
    value = round_ring(value, 1)
    value = round_ring(value, 1)
    pairs = []
    for source in range(lax.axis_size("col")):
        line, place = source // 4, source % 4
        if place != 2:
            pairs.append((source, line * 4 + (place + 1) % 4))
        elif line > 0:
            pairs.append((source, line * 4 - 1))
    return lax.ppermute(value, "col", pairs)


def shards_body(object_field, probe, amplitude, offsets):
    side = probe.shape[1]
    cut = object_field.shape[1] - side // 2
    lower = long_way(object_field[:, cut:, :side])
    upper = passed_along(object_field[:, :side, :side], "col", -1)
    middle = passed_along(object_field[:, side:cut, :side], "col", -1)
    bottom = passed_along(object_field[:, :side, :], "row", -1)
    corner = passed_along(upper, "row", -1)
    count = amplitude.shape[2] * lax.axis_size("row") * lax.axis_size("col")
    main, upper, lower, bottom, corner, probe_acc = all_patches(
        offsets[0, 0], object_field, upper, middle, lower, bottom, corner, probe, amplitude[0, 0], 1.0 / count)
    corner_back = passed_along(corner, "row", 1)
    lower_back = passed_along(lower, "col", 1)
    bottom_back = passed_along(bottom, "row", 1)
    upper_back = passed_along(upper + corner_back, "col", 1)
    probe_total = summed_everywhere(probe_acc)
    right_back = jnp.concatenate([upper_back, lower_back], axis=1)
    main = main.at[:, :side, :].add(bottom_back)
    object_grad = main.at[:, :, :side].add(right_back)
    return (object_grad, probe_total)


def solution(mesh):
    placed = (
        P(None, "row", "col"),
        P(),
        P("row", "col", None, None, None),
        P("row", "col", None, None),
    )
    return jax.shard_map(
        shards_body, mesh=mesh, in_specs=placed, out_specs=(P(None, "row", "col"), P()), check_vma=False
    )
```

```python
import functools
import math

import jax
import jax.numpy as jnp
import numpy as np
from jax import lax
from jax.experimental import pallas as pl
from jax.experimental.pallas import tpu as pltpu
from jax.sharding import PartitionSpec as P


F32 = jnp.float32
BF16 = jnp.bfloat16


def passed_along(value, axis, steps):
    count = lax.axis_size(axis)
    first, last = (max(0, -steps), min(count, count - steps))
    return lax.ppermute(value, axis, [(source, source + steps) for source in range(first, last)])


def split(value):
    high = value.astype(BF16)
    return high, (value - high.astype(F32)).astype(BF16)


def half_tables(size):
    half = size // 2
    tables = []
    for odd in (0, 1):
        angle = ((2 * np.arange(half)[:, None] + odd) * np.arange(half)[None, :] % size) * (2.0 * math.pi / size)
        cosine, sine = np.cos(angle) / math.sqrt(size), np.sin(angle) / math.sqrt(size)
        tables.append(np.block([[cosine, sine], [-sine, cosine]]).astype(np.float32))
    return np.stack(tables)


def split_table(table):
    high = table.astype(BF16)
    return np.stack([high, (table - high.astype(np.float32)).astype(BF16)], axis=1)


def dot(left, right):
    return jnp.dot(left, right, preferred_element_type=F32)


def rolled(block, shift, axis):
    size = block.shape[axis]
    small = 8 if axis == 0 else 128
    count = size // small
    pieces = []
    for index in range(count):
        piece = block[index * small:(index + 1) * small] if axis == 0 else block[:, index * small:(index + 1) * small]
        pieces.append(pltpu.roll(piece, shift, axis))
    place = lax.broadcasted_iota(jnp.int32, pieces[0].shape, axis)
    inside = place >= shift
    out = [jnp.where(inside, pieces[index], pieces[index - 1]) for index in range(count)]
    return jnp.concatenate(out, axis=axis)


def unrolled(block, shift, axis):
    size = block.shape[axis]
    small = 8 if axis == 0 else 128
    count = size // small
    back = lax.rem(small - shift, small)
    pieces = []
    for index in range(count):
        piece = block[index * small:(index + 1) * small] if axis == 0 else block[:, index * small:(index + 1) * small]
        pieces.append(pltpu.roll(piece, back, axis))
    place = lax.broadcasted_iota(jnp.int32, pieces[0].shape, axis)
    inside = place < small - shift
    out = [jnp.where(inside, pieces[index], pieces[(index + 1) % count]) for index in range(count)]
    return jnp.concatenate(out, axis=axis)


def prepare_kernel(off, amp, probe, pick, amp_out, probe_out):
    number = pl.program_id(0)
    side = probe.shape[1]
    half = side // 2
    row, lane = lax.rem(off[number, 0], 8), lax.rem(off[number, 1], 128)
    high, low = split(amp[0])
    high, low = split(dot(high, pick[0]) + dot(low, pick[0]))
    both = dot(pick[1], high) + dot(pick[1], low)
    amp_out[0, 0] = both[:, :half]
    amp_out[0, 1] = both[:, half:]
    for part in (0, 1):
        probe_out[0, part] = rolled(rolled(probe[part], row, 0), lane, 1)


def prepare(off, amp, probe):
    count, side = amp.shape[0], amp.shape[1]
    half = side // 2
    pick = np.zeros((side, side), np.float32)
    pick[2 * np.arange(half), np.arange(half)] = 1.0
    pick[2 * np.arange(half) + 1, half + np.arange(half)] = 1.0
    return pl.pallas_call(
        prepare_kernel,
        grid=(count,),
        out_shape=(jax.ShapeDtypeStruct((count, 2, side, half), F32), jax.ShapeDtypeStruct((count, 2, side, side), F32)),
        in_specs=[pl.BlockSpec(memory_space=pltpu.SMEM),
                  pl.BlockSpec((1, side, side), lambda i: (i, 0, 0)),
                  pl.BlockSpec((2, side, side), lambda i: (0, 0, 0)),
                  pl.BlockSpec((2, side, side), lambda i: (0, 0, 0))],
        out_specs=(pl.BlockSpec((1, 2, side, half), lambda i: (i, 0, 0, 0)),
                   pl.BlockSpec((1, 2, side, side), lambda i: (i, 0, 0, 0))),
    )(off, amp, probe, jnp.asarray(np.stack([pick, pick.T]).astype(BF16)))


def one_patch(top, left, amp, probe, left_table, right_table, ext, grad, probe_acc,
              view, a_high, a_low, x_high, x_low):
    side = probe.shape[1]
    half, step = side // 2, 32
    base_row = pl.multiple_of(top // 8 * 8, 8)
    base_col = pl.multiple_of(left // 128 * 128, 128)
    row, lane = top - base_row, left - base_col
    lanes = lax.broadcasted_iota(jnp.int32, (8, 128), 1)
    in_lane = lanes >= lane
    in_row = lax.broadcasted_iota(jnp.int32, (8, 128), 0) >= row

    def wide(mask, rows):
        return jnp.concatenate([mask] * (rows // 8), axis=0) if rows > 8 else mask

    def tiles(part, offset, rows):
        start = pl.multiple_of(base_row + offset, 8)
        block = ext[part, pl.ds(start, rows), pl.ds(base_col, side + 128)]
        return jnp.where(wide(in_lane, rows), block[:, :128], block[:, side:]), block[:, 128:side]

    def window(part, offset, rows):
        near, far = tiles(part, offset, rows)
        if offset == 0:
            near_end, far_end = tiles(part, side, 8)
            near = jnp.concatenate([jnp.where(in_row, near[:8], near_end), near[8:]], axis=0)
            far = jnp.concatenate([jnp.where(in_row, far[:8], far_end), far[8:]], axis=0)
        out = jnp.concatenate([near, far], axis=1)
        view[part, offset:offset + rows] = out
        return out

    def put(high, low, which, rows, value):
        top_part, rest = split(value)
        high[which, rows] = top_part
        low[which, rows] = rest

    for at in range(0, half, step):
        def wave(offset):
            here = slice(offset, offset + step)
            vr, vi = window(0, offset, step), window(1, offset, step)
            pr, pi = probe[0, here], probe[1, here]
            return pr * vr - pi * vi, pr * vi + pi * vr

        upper_r, upper_i = wave(at)
        lower_r, lower_i = wave(half + at)
        put(a_high, a_low, 0, slice(at, at + step), upper_r + lower_r)
        put(a_high, a_low, 0, slice(half + at, half + at + step), upper_i + lower_i)
        put(a_high, a_low, 1, slice(at, at + step), upper_r - lower_r)
        put(a_high, a_low, 1, slice(half + at, half + at + step), upper_i - lower_i)

    yield

    def left_product(table, odd):
        fine, rough = table[odd, 1], table[odd, 0]
        return dot(jnp.concatenate([rough, rough, fine], axis=1),
                   jnp.concatenate([a_high[odd], a_low[odd], a_high[odd]], axis=0))

    def right_product(table, odd):
        fine, rough = table[odd, 1], table[odd, 0]
        return dot(jnp.concatenate([x_high[odd], x_low[odd], x_high[odd]], axis=1),
                   jnp.concatenate([rough, rough, fine], axis=0))

    for odd in (0, 1):
        out = left_product(left_table, odd)
        for at in range(0, half, step):
            real, imag = out[at:at + step], out[half + at:half + at + step]
            rows = slice(odd * half + at, odd * half + at + step)
            put(x_high, x_low, 0, rows, jnp.concatenate([real[:, :half] + real[:, half:], imag[:, :half] + imag[:, half:]], axis=1))
            put(x_high, x_low, 1, rows, jnp.concatenate([real[:, :half] - real[:, half:], imag[:, :half] - imag[:, half:]], axis=1))
    yield
    for odd in (0, 1):
        far = right_product(right_table, odd)
        for at in range(0, side, step):
            rows = slice(at, at + step)
            real, imag = far[rows, :half], far[rows, half:]
            keep = 1.0 - amp[odd, rows] * lax.rsqrt(jnp.maximum(real * real + imag * imag, 0.25))
            put(x_high, x_low, odd, rows, jnp.concatenate([real * keep, imag * keep], axis=1))
    yield
    even, odd_part = right_product(left_table, 0), right_product(left_table, 1)
    for at in range(0, side, step):
        rows = slice(at, at + step)
        total, difference = even[rows] + odd_part[rows], even[rows] - odd_part[rows]
        which, place = at // half, at % half
        put(a_high, a_low, which, slice(place, place + step), jnp.concatenate([total[:, :half], difference[:, :half]], axis=1))
        put(a_high, a_low, which, slice(half + place, half + place + step), jnp.concatenate([total[:, half:], difference[:, half:]], axis=1))
    yield
    even, odd_part = left_product(right_table, 0), left_product(right_table, 1)

    def add(part, offset, term):
        rows = term.shape[0]
        start = pl.multiple_of(base_row + offset, 8)
        here = wide(in_lane, rows)
        zero = jnp.zeros((rows, 128), F32)
        near, far = term[:, :128], term[:, 128:]
        grad[part, pl.ds(start, rows), pl.ds(base_col, side + 128)] += jnp.concatenate(
            [jnp.where(here, near, zero), far, jnp.where(here, zero, near)], axis=1)

    zero_row = jnp.zeros((8, side), F32)
    both_in_row = jnp.concatenate([in_row] * (side // 128), axis=1)
    for at in range(0, side, step):
        rows = slice(at, at + step)
        place = at % half
        if at < half:
            cr = even[place:place + step] + odd_part[place:place + step]
            ci = even[half + place:half + place + step] + odd_part[half + place:half + place + step]
        else:
            cr = even[place:place + step] - odd_part[place:place + step]
            ci = even[half + place:half + place + step] - odd_part[half + place:half + place + step]
        pr, pi = probe[0, rows], probe[1, rows]
        vr, vi = view[0, rows], view[1, rows]
        for part, term in enumerate((pr * cr + pi * ci, pr * ci - pi * cr)):
            if at == 0:
                add(part, side, jnp.where(both_in_row, zero_row, term[:8]))
                term = jnp.concatenate([jnp.where(both_in_row, term[:8], zero_row), term[8:]], axis=0)
            add(part, at, term)
        view[0, rows] = unrolled(vr * cr + vi * ci, lane, 1)
        view[1, rows] = unrolled(vr * ci - vi * cr, lane, 1)
    yield
    back = lax.rem(8 - row, 8)
    inside = lax.broadcasted_iota(jnp.int32, (8, side), 0) < 8 - row
    for part in (0, 1):
        opening = pltpu.roll(view[part, 0:8], back, 0)
        now = opening
        for at in range(0, side, 8):
            after = opening if at + 8 == side else pltpu.roll(view[part, at + 8:at + 16], back, 0)
            probe_acc[part, at:at + 8] += jnp.where(inside, now, after)
            now = after


def interleaved(patches):
    running = list(patches)
    while running:
        running = [patch for patch in running if next(patch, running) is None]


def patches_kernel(off, tile, upper, middle, lower, bottom, relayed, corner, probe, amp, left_table, right_table,
                   main_out, upper_out, lower_out, bottom_out, corner_out, probe_out, ext, grad, *scratch, scale):
    side = upper.shape[2]
    rows, cols = tile.shape[1], tile.shape[2]
    cut = rows - lower.shape[1]
    number = pl.program_id(0)

    @pl.when(number == 0)
    def opening():
        ext[:, :rows, :cols] = tile[...]
        ext[:, :side, cols:] = upper[...]
        ext[:, side:cut, cols:] = middle[...]
        ext[:, cut:rows, cols:] = lower[...]
        ext[:, rows:, :cols] = bottom[...] + relayed[...]
        ext[:, rows:, cols:] = corner[...]
        grad[...] = jnp.zeros_like(grad)
        probe_out[...] = jnp.zeros_like(probe_out)

    together = amp.shape[0]
    interleaved(
        one_patch(off[number * together + which, 0], off[number * together + which, 1], amp.at[which], probe.at[which],
                  left_table, right_table, ext, grad, probe_out, *[ref.at[which] for ref in scratch])
        for which in range(together))

    @pl.when(number == pl.num_programs(0) - 1)
    def closing():
        main_out[...] = grad[:, :rows, :cols]
        upper_out[...] = grad[:, :side, cols:]
        lower_out[...] = grad[:, side:rows, cols:]
        bottom_out[...] = grad[:, rows:, :cols]
        corner_out[...] = grad[:, rows:, cols:]
        probe_out[...] *= scale


def all_patches(off, tile, upper, middle, lower, bottom, relayed, corner, probe, amp, scale):
    count, side = amp.shape[0], upper.shape[2]
    together = 2 if count % 2 == 0 else 1
    rows, cols = tile.shape[1], tile.shape[2]
    table = half_tables(side)
    tables = [jnp.asarray(split_table(table)), jnp.asarray(split_table(table.transpose(0, 2, 1)))]
    amps, probes = prepare(off, amp, probe)
    vmem = pl.BlockSpec(memory_space=pltpu.VMEM)
    shape = lambda *dims: jax.ShapeDtypeStruct(dims, F32)
    return pl.pallas_call(
        functools.partial(patches_kernel, scale=scale),
        grid=(count // together,),
        out_shape=(shape(2, rows, cols), shape(2, side, side), shape(2, rows - side, side), shape(2, side, cols),
                   shape(2, side, side), shape(2, side, side)),
        in_specs=[pl.BlockSpec(memory_space=pltpu.SMEM)] + [vmem] * 7
                 + [pl.BlockSpec((together, 2, side, side), lambda i: (i, 0, 0, 0)),
                    pl.BlockSpec((together, 2, side, side // 2), lambda i: (i, 0, 0, 0))] + [vmem] * 2,
        out_specs=[vmem] * 6,
        scratch_shapes=[pltpu.VMEM((2, rows + side, cols + side), F32)] * 2
                     + [pltpu.VMEM((together, 2, side, side), F32)] + [pltpu.VMEM((together, 2, side, side), BF16)] * 4,
        compiler_params=pltpu.CompilerParams(vmem_limit_bytes=50 * 1024 * 1024),
    )(off, tile, upper, middle, lower, bottom, relayed, corner, probes, amps, *tables)


ACROSS, LINES = (2, 4, 6), (4, 8, 12)


def exchanged(pieces, distances, axis):
    return [lax.ppermute(piece, axis, [(i, i ^ distance) for i in range(lax.axis_size(axis))])
            for piece, distance in zip(pieces, distances)]


def added(parts):
    while len(parts) > 1:
        parts = [parts[i] + parts[i + 1] for i in range(0, len(parts), 2)]
    return parts[0]


def scattered(value, me, distances, axis):
    rows = value.shape[0] // 4
    pieces = [lax.dynamic_slice_in_dim(value, (me ^ place) * rows, rows, 0) for place in range(4)]
    return added(pieces[:1] + exchanged(pieces[1:], distances, axis))


def everywhere(value, distances, axis):
    return added([value] + exchanged([value] * 3, distances, axis))


def gathered(value, me, distances, axis):
    rows = value.shape[0]
    whole = jnp.zeros((rows * 4, value.shape[1]), value.dtype)
    for place, part in enumerate([value] + exchanged([value] * 3, distances, axis)):
        whole = lax.dynamic_update_slice_in_dim(whole, part, (me ^ place) * rows, 0)
    return whole


def halved(value, distance, axis):
    rows = value.shape[0] // 2
    upper = (lax.axis_index(axis) & distance) != 0
    low, high = value[:rows], value[rows:]
    got, = exchanged([jnp.where(upper, low, high)], (distance,), axis)
    return jnp.where(upper, high, low) + got


def doubled(value, distance, axis):
    upper = (lax.axis_index(axis) & distance) != 0
    got, = exchanged([value], (distance,), axis)
    return jnp.concatenate([jnp.where(upper, got, value), jnp.where(upper, value, got)], axis=0)


def round_ring(value, step):
    size = lax.axis_size("col")
    return lax.ppermute(value, "col", [(i, i // 4 * 4 + (i + step) % 4) for i in range(size)])


def summed_everywhere(value):
    shape = value.shape
    value = value.reshape(-1, shape[-1])
    chip = (lax.axis_index("row") >> 1) & 3
    value = halved(value, 1, "row")
    value = scattered(value, chip, ACROSS, "row")
    value = everywhere(value, LINES, "col")
    value = value + exchanged([value], (8,), "row")[0]
    value = everywhere(value, (1, 2, 3), "col")
    value = gathered(value, chip, ACROSS, "row")
    value = doubled(value, 1, "row")
    return value.reshape(shape)


def long_way(value):
    value = round_ring(value, 1)
    value = round_ring(value, 1)
    pairs = []
    for source in range(lax.axis_size("col")):
        line, place = source // 4, source % 4
        if place != 2:
            pairs.append((source, line * 4 + (place + 1) % 4))
        elif line > 0:
            pairs.append((source, line * 4 - 1))
    return lax.ppermute(value, "col", pairs)


def bottom_rows(value):
    count = lax.axis_size("row")
    half = count // 2
    relayed = lax.ppermute(value, "row", [(half, count - 2)])
    bottom = lax.ppermute(value, "row", [(i, i - 1) for i in range(1, count) if i != half])
    return bottom, lax.ppermute(relayed, "row", [(count - 2, half - 1)])


def shards_body(object_field, probe, amplitude, offsets):
    side = probe.shape[1]
    cut = object_field.shape[1] - side * 7 // 16
    lower = long_way(object_field[:, cut:, :side])
    upper = passed_along(object_field[:, :side, :side], "col", -1)
    middle = passed_along(object_field[:, side:cut, :side], "col", -1)
    bottom, relayed = bottom_rows(object_field[:, :side, :])
    corner = passed_along(upper, "row", -1)
    count = amplitude.shape[2] * lax.axis_size("row") * lax.axis_size("col")
    main, upper, lower, bottom, corner, probe_acc = all_patches(
        offsets[0, 0], object_field, upper, middle, lower, bottom, relayed, corner, probe, amplitude[0, 0], 1.0 / count)
    corner_back = passed_along(corner, "row", 1)
    lower_back = passed_along(lower, "col", 1)
    bottom_back = passed_along(bottom, "row", 1)
    upper_back = passed_along(upper + corner_back, "col", 1)
    probe_total = summed_everywhere(probe_acc)
    right_back = jnp.concatenate([upper_back, lower_back], axis=1)
    main = main.at[:, :side, :].add(bottom_back)
    object_grad = main.at[:, :, :side].add(right_back)
    return (object_grad, probe_total)


def solution(mesh):
    placed = (
        P(None, "row", "col"),
        P(),
        P("row", "col", None, None, None),
        P("row", "col", None, None),
    )
    return jax.shard_map(
        shards_body, mesh=mesh, in_specs=placed, out_specs=(P(None, "row", "col"), P()), check_vma=False
    )
```

```python
import functools
import math

import jax
import jax.numpy as jnp
import numpy as np
from jax import lax
from jax.experimental import pallas as pl
from jax.experimental.pallas import tpu as pltpu
from jax.sharding import PartitionSpec as P


F32 = jnp.float32
BF16 = jnp.bfloat16


def passed_along(value, axis, steps):
    count = lax.axis_size(axis)
    first, last = (max(0, -steps), min(count, count - steps))
    return lax.ppermute(value, axis, [(source, source + steps) for source in range(first, last)])


def split(value):
    high = value.astype(BF16)
    return high, (value - high.astype(F32)).astype(BF16)


def half_tables(size):
    half = size // 2
    tables = []
    for odd in (0, 1):
        angle = ((2 * np.arange(half)[:, None] + odd) * np.arange(half)[None, :] % size) * (2.0 * math.pi / size)
        cosine, sine = np.cos(angle) / math.sqrt(size), np.sin(angle) / math.sqrt(size)
        tables.append(np.block([[cosine, sine], [-sine, cosine]]).astype(np.float32))
    return np.stack(tables)


def split_table(table):
    high = table.astype(BF16)
    return np.stack([high, (table - high.astype(np.float32)).astype(BF16)], axis=1)


def dot(left, right):
    return jnp.dot(left, right, preferred_element_type=F32)


def rolled(block, shift, axis):
    size = block.shape[axis]
    small = 8 if axis == 0 else 128
    count = size // small
    pieces = []
    for index in range(count):
        piece = block[index * small:(index + 1) * small] if axis == 0 else block[:, index * small:(index + 1) * small]
        pieces.append(pltpu.roll(piece, shift, axis))
    place = lax.broadcasted_iota(jnp.int32, pieces[0].shape, axis)
    inside = place >= shift
    out = [jnp.where(inside, pieces[index], pieces[index - 1]) for index in range(count)]
    return jnp.concatenate(out, axis=axis)


def unrolled(block, shift, axis):
    size = block.shape[axis]
    small = 8 if axis == 0 else 128
    count = size // small
    back = lax.rem(small - shift, small)
    pieces = []
    for index in range(count):
        piece = block[index * small:(index + 1) * small] if axis == 0 else block[:, index * small:(index + 1) * small]
        pieces.append(pltpu.roll(piece, back, axis))
    place = lax.broadcasted_iota(jnp.int32, pieces[0].shape, axis)
    inside = place < small - shift
    out = [jnp.where(inside, pieces[index], pieces[(index + 1) % count]) for index in range(count)]
    return jnp.concatenate(out, axis=axis)


def prepare_kernel(off, amp, probe, pick, amp_out, probe_out):
    number = pl.program_id(0)
    side = probe.shape[1]
    half = side // 2
    row, lane = lax.rem(off[number, 0], 8), lax.rem(off[number, 1], 128)
    high, low = split(amp[0])
    high, low = split(dot(high, pick[0]) + dot(low, pick[0]))
    both = dot(pick[1], high) + dot(pick[1], low)
    amp_out[0, 0] = both[:, :half]
    amp_out[0, 1] = both[:, half:]
    for part in (0, 1):
        probe_out[0, part] = rolled(rolled(probe[part], row, 0), lane, 1)


def prepare(off, amp, probe):
    count, side = amp.shape[0], amp.shape[1]
    half = side // 2
    pick = np.zeros((side, side), np.float32)
    pick[2 * np.arange(half), np.arange(half)] = 1.0
    pick[2 * np.arange(half) + 1, half + np.arange(half)] = 1.0
    return pl.pallas_call(
        prepare_kernel,
        grid=(count,),
        out_shape=(jax.ShapeDtypeStruct((count, 2, side, half), F32), jax.ShapeDtypeStruct((count, 2, side, side), F32)),
        in_specs=[pl.BlockSpec(memory_space=pltpu.SMEM),
                  pl.BlockSpec((1, side, side), lambda i: (i, 0, 0)),
                  pl.BlockSpec((2, side, side), lambda i: (0, 0, 0)),
                  pl.BlockSpec((2, side, side), lambda i: (0, 0, 0))],
        out_specs=(pl.BlockSpec((1, 2, side, half), lambda i: (i, 0, 0, 0)),
                   pl.BlockSpec((1, 2, side, side), lambda i: (i, 0, 0, 0))),
    )(off, amp, probe, jnp.asarray(np.stack([pick, pick.T]).astype(BF16)))


def one_patch(top, left, amp, probe, left_table, right_table, ext, grad, probe_acc,
              view, a_high, a_low, x_high, x_low):
    side = probe.shape[1]
    half, step = side // 2, 32
    base_row = pl.multiple_of(top // 8 * 8, 8)
    base_col = pl.multiple_of(left // 128 * 128, 128)
    row, lane = top - base_row, left - base_col
    lanes = lax.broadcasted_iota(jnp.int32, (8, 128), 1)
    in_lane = lanes >= lane
    in_row = lax.broadcasted_iota(jnp.int32, (8, 128), 0) >= row

    def wide(mask, rows):
        return jnp.concatenate([mask] * (rows // 8), axis=0) if rows > 8 else mask

    def tiles(part, offset, rows):
        start = pl.multiple_of(base_row + offset, 8)
        block = ext[part, pl.ds(start, rows), pl.ds(base_col, side + 128)]
        return jnp.where(wide(in_lane, rows), block[:, :128], block[:, side:]), block[:, 128:side]

    def window(part, offset, rows):
        near, far = tiles(part, offset, rows)
        if offset == 0:
            near_end, far_end = tiles(part, side, 8)
            near = jnp.concatenate([jnp.where(in_row, near[:8], near_end), near[8:]], axis=0)
            far = jnp.concatenate([jnp.where(in_row, far[:8], far_end), far[8:]], axis=0)
        out = jnp.concatenate([near, far], axis=1)
        view[part, offset:offset + rows] = out
        return out

    def put(high, low, which, rows, value):
        top_part, rest = split(value)
        high[which, rows] = top_part
        low[which, rows] = rest

    for at in range(0, half, step):
        def wave(offset):
            here = slice(offset, offset + step)
            vr, vi = window(0, offset, step), window(1, offset, step)
            pr, pi = probe[0, here], probe[1, here]
            return pr * vr - pi * vi, pr * vi + pi * vr

        upper_r, upper_i = wave(at)
        lower_r, lower_i = wave(half + at)
        put(a_high, a_low, 0, slice(at, at + step), upper_r + lower_r)
        put(a_high, a_low, 0, slice(half + at, half + at + step), upper_i + lower_i)
        put(a_high, a_low, 1, slice(at, at + step), upper_r - lower_r)
        put(a_high, a_low, 1, slice(half + at, half + at + step), upper_i - lower_i)

    yield

    def left_product(table, odd):
        fine, rough = table[odd, 1], table[odd, 0]
        return dot(jnp.concatenate([rough, rough, fine], axis=1),
                   jnp.concatenate([a_high[odd], a_low[odd], a_high[odd]], axis=0))

    def right_product(table, odd):
        fine, rough = table[odd, 1], table[odd, 0]
        return dot(jnp.concatenate([x_high[odd], x_low[odd], x_high[odd]], axis=1),
                   jnp.concatenate([rough, rough, fine], axis=0))

    for odd in (0, 1):
        out = left_product(left_table, odd)
        for at in range(0, half, step):
            real, imag = out[at:at + step], out[half + at:half + at + step]
            rows = slice(odd * half + at, odd * half + at + step)
            put(x_high, x_low, 0, rows, jnp.concatenate([real[:, :half] + real[:, half:], imag[:, :half] + imag[:, half:]], axis=1))
            put(x_high, x_low, 1, rows, jnp.concatenate([real[:, :half] - real[:, half:], imag[:, :half] - imag[:, half:]], axis=1))
    yield
    for odd in (0, 1):
        far = right_product(right_table, odd)
        for at in range(0, side, step):
            rows = slice(at, at + step)
            real, imag = far[rows, :half], far[rows, half:]
            keep = 1.0 - amp[odd, rows] * lax.rsqrt(jnp.maximum(real * real + imag * imag, 0.25))
            put(x_high, x_low, odd, rows, jnp.concatenate([real * keep, imag * keep], axis=1))
    yield
    even, odd_part = right_product(left_table, 0), right_product(left_table, 1)
    for at in range(0, side, step):
        rows = slice(at, at + step)
        total, difference = even[rows] + odd_part[rows], even[rows] - odd_part[rows]
        which, place = at // half, at % half
        put(a_high, a_low, which, slice(place, place + step), jnp.concatenate([total[:, :half], difference[:, :half]], axis=1))
        put(a_high, a_low, which, slice(half + place, half + place + step), jnp.concatenate([total[:, half:], difference[:, half:]], axis=1))
    yield
    even, odd_part = left_product(right_table, 0), left_product(right_table, 1)

    def add(part, offset, term):
        rows = term.shape[0]
        start = pl.multiple_of(base_row + offset, 8)
        here = wide(in_lane, rows)
        zero = jnp.zeros((rows, 128), F32)
        near, far = term[:, :128], term[:, 128:]
        grad[part, pl.ds(start, rows), pl.ds(base_col, side + 128)] += jnp.concatenate(
            [jnp.where(here, near, zero), far, jnp.where(here, zero, near)], axis=1)

    zero_row = jnp.zeros((8, side), F32)
    both_in_row = jnp.concatenate([in_row] * (side // 128), axis=1)
    for at in range(0, side, step):
        rows = slice(at, at + step)
        place = at % half
        if at < half:
            cr = even[place:place + step] + odd_part[place:place + step]
            ci = even[half + place:half + place + step] + odd_part[half + place:half + place + step]
        else:
            cr = even[place:place + step] - odd_part[place:place + step]
            ci = even[half + place:half + place + step] - odd_part[half + place:half + place + step]
        pr, pi = probe[0, rows], probe[1, rows]
        vr, vi = view[0, rows], view[1, rows]
        for part, term in enumerate((pr * cr + pi * ci, pr * ci - pi * cr)):
            if at == 0:
                add(part, side, jnp.where(both_in_row, zero_row, term[:8]))
                term = jnp.concatenate([jnp.where(both_in_row, term[:8], zero_row), term[8:]], axis=0)
            add(part, at, term)
        view[0, rows] = unrolled(vr * cr + vi * ci, lane, 1)
        view[1, rows] = unrolled(vr * ci - vi * cr, lane, 1)
    yield
    back = lax.rem(8 - row, 8)
    inside = lax.broadcasted_iota(jnp.int32, (8, side), 0) < 8 - row
    for part in (0, 1):
        opening = pltpu.roll(view[part, 0:8], back, 0)
        now = opening
        for at in range(0, side, 8):
            after = opening if at + 8 == side else pltpu.roll(view[part, at + 8:at + 16], back, 0)
            probe_acc[part, at:at + 8] += jnp.where(inside, now, after)
            now = after


def interleaved(patches):
    running = list(patches)
    while running:
        running = [patch for patch in running if next(patch, running) is None]


def patches_kernel(off, tile, upper, middle, lower, bottom, deeper, relayed, corner, probe, amp, left_table, right_table,
                   main_out, upper_out, lower_out, bottom_out, corner_out, probe_out, ext, grad, *scratch, scale):
    side = upper.shape[2]
    rows, cols = tile.shape[1], tile.shape[2]
    cut = rows - lower.shape[1]
    number = pl.program_id(0)

    @pl.when(number == 0)
    def opening():
        ext[:, :rows, :cols] = tile[...]
        ext[:, :side, cols:] = upper[...]
        ext[:, side:cut, cols:] = middle[...]
        ext[:, cut:rows, cols:] = lower[...]
        ext[:, rows:rows + side // 2, :cols] = bottom[...]
        ext[:, rows + side // 2:, :cols] = deeper[...] + relayed[...]
        ext[:, rows:, cols:] = corner[...]
        grad[...] = jnp.zeros_like(grad)
        probe_out[...] = jnp.zeros_like(probe_out)

    together = amp.shape[0]
    interleaved(
        one_patch(off[number * together + which, 0], off[number * together + which, 1], amp.at[which], probe.at[which],
                  left_table, right_table, ext, grad, probe_out, *[ref.at[which] for ref in scratch])
        for which in range(together))

    @pl.when(number == pl.num_programs(0) - 1)
    def closing():
        main_out[...] = grad[:, :rows, :cols]
        upper_out[...] = grad[:, :side, cols:]
        lower_out[...] = grad[:, side:rows, cols:]
        bottom_out[...] = grad[:, rows:, :cols]
        corner_out[...] = grad[:, rows:, cols:]
        probe_out[...] *= scale


def all_patches(off, tile, upper, middle, lower, bottom, deeper, relayed, corner, probe, amp, scale):
    count, side = amp.shape[0], upper.shape[2]
    together = 2 if count % 2 == 0 else 1
    rows, cols = tile.shape[1], tile.shape[2]
    table = half_tables(side)
    tables = [jnp.asarray(split_table(table)), jnp.asarray(split_table(table.transpose(0, 2, 1)))]
    amps, probes = prepare(off, amp, probe)
    vmem = pl.BlockSpec(memory_space=pltpu.VMEM)
    shape = lambda *dims: jax.ShapeDtypeStruct(dims, F32)
    return pl.pallas_call(
        functools.partial(patches_kernel, scale=scale),
        grid=(count // together,),
        out_shape=(shape(2, rows, cols), shape(2, side, side), shape(2, rows - side, side), shape(2, side, cols),
                   shape(2, side, side), shape(2, side, side)),
        in_specs=[pl.BlockSpec(memory_space=pltpu.SMEM)] + [vmem] * 8
                 + [pl.BlockSpec((together, 2, side, side), lambda i: (i, 0, 0, 0)),
                    pl.BlockSpec((together, 2, side, side // 2), lambda i: (i, 0, 0, 0))] + [vmem] * 2,
        out_specs=[vmem] * 6,
        scratch_shapes=[pltpu.VMEM((2, rows + side, cols + side), F32)] * 2
                     + [pltpu.VMEM((together, 2, side, side), F32)] + [pltpu.VMEM((together, 2, side, side), BF16)] * 4,
        compiler_params=pltpu.CompilerParams(vmem_limit_bytes=50 * 1024 * 1024),
    )(off, tile, upper, middle, lower, bottom, deeper, relayed, corner, probes, amps, *tables)


ACROSS, LINES = (2, 4, 6), (4, 8, 12)


def exchanged(pieces, distances, axis):
    return [lax.ppermute(piece, axis, [(i, i ^ distance) for i in range(lax.axis_size(axis))])
            for piece, distance in zip(pieces, distances)]


def added(parts):
    while len(parts) > 1:
        parts = [parts[i] + parts[i + 1] for i in range(0, len(parts), 2)]
    return parts[0]


def scattered(value, me, distances, axis):
    rows = value.shape[0] // 4
    pieces = [lax.dynamic_slice_in_dim(value, (me ^ place) * rows, rows, 0) for place in range(4)]
    return added(pieces[:1] + exchanged(pieces[1:], distances, axis))


def everywhere(value, distances, axis):
    return added([value] + exchanged([value] * 3, distances, axis))


def gathered(value, me, distances, axis):
    rows = value.shape[0]
    whole = jnp.zeros((rows * 4, value.shape[1]), value.dtype)
    for place, part in enumerate([value] + exchanged([value] * 3, distances, axis)):
        whole = lax.dynamic_update_slice_in_dim(whole, part, (me ^ place) * rows, 0)
    return whole


def halved(value, distance, axis):
    rows = value.shape[0] // 2
    upper = (lax.axis_index(axis) & distance) != 0
    low, high = value[:rows], value[rows:]
    got, = exchanged([jnp.where(upper, low, high)], (distance,), axis)
    return jnp.where(upper, high, low) + got


def doubled(value, distance, axis):
    upper = (lax.axis_index(axis) & distance) != 0
    got, = exchanged([value], (distance,), axis)
    return jnp.concatenate([jnp.where(upper, got, value), jnp.where(upper, value, got)], axis=0)


def round_ring(value, step):
    size = lax.axis_size("col")
    return lax.ppermute(value, "col", [(i, i // 4 * 4 + (i + step) % 4) for i in range(size)])


def summed_everywhere(value):
    shape = value.shape
    value = value.reshape(-1, shape[-1])
    chip = (lax.axis_index("row") >> 1) & 3
    value = halved(value, 1, "row")
    value = scattered(value, chip, ACROSS, "row")
    value = everywhere(value, LINES, "col")
    value = value + exchanged([value], (8,), "row")[0]
    value = everywhere(value, (1, 2, 3), "col")
    value = gathered(value, chip, ACROSS, "row")
    value = doubled(value, 1, "row")
    return value.reshape(shape)


def long_way(value):
    value = round_ring(value, 1)
    value = round_ring(value, 1)
    pairs = []
    for source in range(lax.axis_size("col")):
        line, place = source // 4, source % 4
        if place != 2:
            pairs.append((source, line * 4 + (place + 1) % 4))
        elif line > 0:
            pairs.append((source, line * 4 - 1))
    return lax.ppermute(value, "col", pairs)


def deeper_rows(value):
    count = lax.axis_size("row")
    half = count // 2
    relayed = lax.ppermute(value, "row", [(half, count - 2)])
    deeper = lax.ppermute(value, "row", [(i, i - 1) for i in range(1, count) if i != half])
    return deeper, lax.ppermute(relayed, "row", [(count - 2, half - 1)])


def shards_body(object_field, probe, amplitude, offsets):
    side = probe.shape[1]
    cut = object_field.shape[1] - side // 2
    lower = long_way(object_field[:, cut:, :side])
    upper = passed_along(object_field[:, :side, :side], "col", -1)
    middle = passed_along(object_field[:, side:cut, :side], "col", -1)
    bottom = passed_along(object_field[:, :side // 2, :], "row", -1)
    deeper, relayed = deeper_rows(object_field[:, side // 2:side, :])
    corner = passed_along(upper, "row", -1)
    count = amplitude.shape[2] * lax.axis_size("row") * lax.axis_size("col")
    main, upper, lower, bottom, corner, probe_acc = all_patches(
        offsets[0, 0], object_field, upper, middle, lower, bottom, deeper, relayed, corner, probe, amplitude[0, 0], 1.0 / count)
    corner_back = passed_along(corner, "row", 1)
    lower_back = passed_along(lower, "col", 1)
    bottom_back = passed_along(bottom, "row", 1)
    upper_back = passed_along(upper + corner_back, "col", 1)
    probe_total = summed_everywhere(probe_acc)
    right_back = jnp.concatenate([upper_back, lower_back], axis=1)
    main = main.at[:, :side, :].add(bottom_back)
    object_grad = main.at[:, :, :side].add(right_back)
    return (object_grad, probe_total)


def solution(mesh):
    placed = (
        P(None, "row", "col"),
        P(),
        P("row", "col", None, None, None),
        P("row", "col", None, None),
    )
    return jax.shard_map(
        shards_body, mesh=mesh, in_specs=placed, out_specs=(P(None, "row", "col"), P()), check_vma=False
    )
```

```python
import functools
import math

import jax
import jax.numpy as jnp
import numpy as np
from jax import lax
from jax.experimental import pallas as pl
from jax.experimental.pallas import tpu as pltpu
from jax.sharding import PartitionSpec as P


F32 = jnp.float32
BF16 = jnp.bfloat16


def passed_along(value, axis, steps):
    count = lax.axis_size(axis)
    first, last = (max(0, -steps), min(count, count - steps))
    return lax.ppermute(value, axis, [(source, source + steps) for source in range(first, last)])


def split(value):
    high = value.astype(BF16)
    return high, (value - high.astype(F32)).astype(BF16)


def half_tables(size):
    half = size // 2
    tables = []
    for odd in (0, 1):
        angle = ((2 * np.arange(half)[:, None] + odd) * np.arange(half)[None, :] % size) * (2.0 * math.pi / size)
        cosine, sine = np.cos(angle) / math.sqrt(size), np.sin(angle) / math.sqrt(size)
        tables.append(np.block([[cosine, sine], [-sine, cosine]]).astype(np.float32))
    return np.stack(tables)


def split_table(table):
    high = table.astype(BF16)
    return np.stack([high, (table - high.astype(np.float32)).astype(BF16)], axis=1)


def dot(left, right):
    return jnp.dot(left, right, preferred_element_type=F32)


def rolled(block, shift, axis):
    size = block.shape[axis]
    small = 8 if axis == 0 else 128
    count = size // small
    pieces = []
    for index in range(count):
        piece = block[index * small:(index + 1) * small] if axis == 0 else block[:, index * small:(index + 1) * small]
        pieces.append(pltpu.roll(piece, shift, axis))
    place = lax.broadcasted_iota(jnp.int32, pieces[0].shape, axis)
    inside = place >= shift
    out = [jnp.where(inside, pieces[index], pieces[index - 1]) for index in range(count)]
    return jnp.concatenate(out, axis=axis)


def unrolled(block, shift, axis):
    size = block.shape[axis]
    small = 8 if axis == 0 else 128
    count = size // small
    back = lax.rem(small - shift, small)
    pieces = []
    for index in range(count):
        piece = block[index * small:(index + 1) * small] if axis == 0 else block[:, index * small:(index + 1) * small]
        pieces.append(pltpu.roll(piece, back, axis))
    place = lax.broadcasted_iota(jnp.int32, pieces[0].shape, axis)
    inside = place < small - shift
    out = [jnp.where(inside, pieces[index], pieces[(index + 1) % count]) for index in range(count)]
    return jnp.concatenate(out, axis=axis)


def prepare_kernel(off, amp, probe, pick, amp_out, probe_out):
    number = pl.program_id(0)
    side = probe.shape[1]
    half = side // 2
    row, lane = lax.rem(off[number, 0], 8), lax.rem(off[number, 1], 128)
    high, low = split(amp[0])
    high, low = split(dot(high, pick[0]) + dot(low, pick[0]))
    both = dot(pick[1], high) + dot(pick[1], low)
    amp_out[0, 0] = both[:, :half]
    amp_out[0, 1] = both[:, half:]
    for part in (0, 1):
        probe_out[0, part] = rolled(rolled(probe[part], row, 0), lane, 1)


def prepare(off, amp, probe):
    count, side = amp.shape[0], amp.shape[1]
    half = side // 2
    pick = np.zeros((side, side), np.float32)
    pick[2 * np.arange(half), np.arange(half)] = 1.0
    pick[2 * np.arange(half) + 1, half + np.arange(half)] = 1.0
    return pl.pallas_call(
        prepare_kernel,
        grid=(count,),
        out_shape=(jax.ShapeDtypeStruct((count, 2, side, half), F32), jax.ShapeDtypeStruct((count, 2, side, side), F32)),
        in_specs=[pl.BlockSpec(memory_space=pltpu.SMEM),
                  pl.BlockSpec((1, side, side), lambda i: (i, 0, 0)),
                  pl.BlockSpec((2, side, side), lambda i: (0, 0, 0)),
                  pl.BlockSpec((2, side, side), lambda i: (0, 0, 0))],
        out_specs=(pl.BlockSpec((1, 2, side, half), lambda i: (i, 0, 0, 0)),
                   pl.BlockSpec((1, 2, side, side), lambda i: (i, 0, 0, 0))),
    )(off, amp, probe, jnp.asarray(np.stack([pick, pick.T]).astype(BF16)))


def one_patch(top, left, amp, probe, left_table, right_table, ext, grad, probe_acc,
              view, a_high, a_low, x_high, x_low):
    side = probe.shape[1]
    half, step = side // 2, 32
    base_row = pl.multiple_of(top // 8 * 8, 8)
    base_col = pl.multiple_of(left // 128 * 128, 128)
    row, lane = top - base_row, left - base_col
    lanes = lax.broadcasted_iota(jnp.int32, (8, 128), 1)
    in_lane = lanes >= lane
    in_row = lax.broadcasted_iota(jnp.int32, (8, 128), 0) >= row

    def wide(mask, rows):
        return jnp.concatenate([mask] * (rows // 8), axis=0) if rows > 8 else mask

    def tiles(part, offset, rows):
        start = pl.multiple_of(base_row + offset, 8)
        block = ext[part, pl.ds(start, rows), pl.ds(base_col, side + 128)]
        return jnp.where(wide(in_lane, rows), block[:, :128], block[:, side:]), block[:, 128:side]

    def window(part, offset, rows):
        near, far = tiles(part, offset, rows)
        if offset == 0:
            near_end, far_end = tiles(part, side, 8)
            near = jnp.concatenate([jnp.where(in_row, near[:8], near_end), near[8:]], axis=0)
            far = jnp.concatenate([jnp.where(in_row, far[:8], far_end), far[8:]], axis=0)
        out = jnp.concatenate([near, far], axis=1)
        view[part, offset:offset + rows] = out
        return out

    def put(high, low, which, rows, value):
        top_part, rest = split(value)
        high[which, rows] = top_part
        low[which, rows] = rest

    for at in range(0, half, step):
        def wave(offset):
            here = slice(offset, offset + step)
            vr, vi = window(0, offset, step), window(1, offset, step)
            pr, pi = probe[0, here], probe[1, here]
            return pr * vr - pi * vi, pr * vi + pi * vr

        upper_r, upper_i = wave(at)
        lower_r, lower_i = wave(half + at)
        put(a_high, a_low, 0, slice(at, at + step), upper_r + lower_r)
        put(a_high, a_low, 0, slice(half + at, half + at + step), upper_i + lower_i)
        put(a_high, a_low, 1, slice(at, at + step), upper_r - lower_r)
        put(a_high, a_low, 1, slice(half + at, half + at + step), upper_i - lower_i)

    yield

    def left_product(table, odd):
        fine, rough = table[odd, 1], table[odd, 0]
        return dot(jnp.concatenate([rough, rough, fine], axis=1),
                   jnp.concatenate([a_high[odd], a_low[odd], a_high[odd]], axis=0))

    def right_product(table, odd):
        fine, rough = table[odd, 1], table[odd, 0]
        return dot(jnp.concatenate([x_high[odd], x_low[odd], x_high[odd]], axis=1),
                   jnp.concatenate([rough, rough, fine], axis=0))

    for odd in (0, 1):
        out = left_product(left_table, odd)
        for at in range(0, half, step):
            real, imag = out[at:at + step], out[half + at:half + at + step]
            rows = slice(odd * half + at, odd * half + at + step)
            put(x_high, x_low, 0, rows, jnp.concatenate([real[:, :half] + real[:, half:], imag[:, :half] + imag[:, half:]], axis=1))
            put(x_high, x_low, 1, rows, jnp.concatenate([real[:, :half] - real[:, half:], imag[:, :half] - imag[:, half:]], axis=1))
    yield
    for odd in (0, 1):
        far = right_product(right_table, odd)
        for at in range(0, side, step):
            rows = slice(at, at + step)
            real, imag = far[rows, :half], far[rows, half:]
            keep = 1.0 - amp[odd, rows] * lax.rsqrt(jnp.maximum(real * real + imag * imag, 0.25))
            put(x_high, x_low, odd, rows, jnp.concatenate([real * keep, imag * keep], axis=1))
    yield
    even, odd_part = right_product(left_table, 0), right_product(left_table, 1)
    for at in range(0, side, step):
        rows = slice(at, at + step)
        total, difference = even[rows] + odd_part[rows], even[rows] - odd_part[rows]
        which, place = at // half, at % half
        put(a_high, a_low, which, slice(place, place + step), jnp.concatenate([total[:, :half], difference[:, :half]], axis=1))
        put(a_high, a_low, which, slice(half + place, half + place + step), jnp.concatenate([total[:, half:], difference[:, half:]], axis=1))
    yield
    even, odd_part = left_product(right_table, 0), left_product(right_table, 1)

    def add(part, offset, term):
        rows = term.shape[0]
        start = pl.multiple_of(base_row + offset, 8)
        here = wide(in_lane, rows)
        zero = jnp.zeros((rows, 128), F32)
        near, far = term[:, :128], term[:, 128:]
        grad[part, pl.ds(start, rows), pl.ds(base_col, side + 128)] += jnp.concatenate(
            [jnp.where(here, near, zero), far, jnp.where(here, zero, near)], axis=1)

    zero_row = jnp.zeros((8, side), F32)
    both_in_row = jnp.concatenate([in_row] * (side // 128), axis=1)
    for at in range(0, side, step):
        rows = slice(at, at + step)
        place = at % half
        if at < half:
            cr = even[place:place + step] + odd_part[place:place + step]
            ci = even[half + place:half + place + step] + odd_part[half + place:half + place + step]
        else:
            cr = even[place:place + step] - odd_part[place:place + step]
            ci = even[half + place:half + place + step] - odd_part[half + place:half + place + step]
        pr, pi = probe[0, rows], probe[1, rows]
        vr, vi = view[0, rows], view[1, rows]
        for part, term in enumerate((pr * cr + pi * ci, pr * ci - pi * cr)):
            if at == 0:
                add(part, side, jnp.where(both_in_row, zero_row, term[:8]))
                term = jnp.concatenate([jnp.where(both_in_row, term[:8], zero_row), term[8:]], axis=0)
            add(part, at, term)
        view[0, rows] = unrolled(vr * cr + vi * ci, lane, 1)
        view[1, rows] = unrolled(vr * ci - vi * cr, lane, 1)
    yield
    back = lax.rem(8 - row, 8)
    inside = lax.broadcasted_iota(jnp.int32, (8, side), 0) < 8 - row
    for part in (0, 1):
        opening = pltpu.roll(view[part, 0:8], back, 0)
        now = opening
        for at in range(0, side, 8):
            after = opening if at + 8 == side else pltpu.roll(view[part, at + 8:at + 16], back, 0)
            probe_acc[part, at:at + 8] += jnp.where(inside, now, after)
            now = after


def interleaved(patches):
    running = list(patches)
    while running:
        running = [patch for patch in running if next(patch, running) is None]


def patches_kernel(off, tile, upper, middle, lower, bottom, deeper, relayed, corner, probe, amp, left_table, right_table,
                   main_out, upper_out, lower_out, bottom_out, deeper_out, corner_out, probe_out, ext, grad, *scratch, scale):
    side = upper.shape[2]
    rows, cols = tile.shape[1], tile.shape[2]
    cut = rows - lower.shape[1]
    number = pl.program_id(0)

    @pl.when(number == 0)
    def opening():
        ext[:, :rows, :cols] = tile[...]
        ext[:, :side, cols:] = upper[...]
        ext[:, side:cut, cols:] = middle[...]
        ext[:, cut:rows, cols:] = lower[...]
        ext[:, rows:rows + side // 2, :cols] = bottom[...]
        ext[:, rows + side // 2:, :cols] = deeper[...] + relayed[...]
        ext[:, rows:, cols:] = corner[...]
        grad[...] = jnp.zeros_like(grad)
        probe_out[...] = jnp.zeros_like(probe_out)

    together = amp.shape[0]
    interleaved(
        one_patch(off[number * together + which, 0], off[number * together + which, 1], amp.at[which], probe.at[which],
                  left_table, right_table, ext, grad, probe_out, *[ref.at[which] for ref in scratch])
        for which in range(together))

    @pl.when(number == pl.num_programs(0) - 1)
    def closing():
        main_out[...] = grad[:, :rows, :cols]
        upper_out[...] = grad[:, :side, cols:]
        lower_out[...] = grad[:, side:rows, cols:]
        bottom_out[...] = grad[:, rows:rows + side // 2, :cols]
        deeper_out[...] = grad[:, rows + side // 2:, :cols]
        corner_out[...] = grad[:, rows:, cols:]
        probe_out[...] *= scale


def all_patches(off, tile, upper, middle, lower, bottom, deeper, relayed, corner, probe, amp, scale):
    count, side = amp.shape[0], upper.shape[2]
    together = 2 if count % 2 == 0 else 1
    rows, cols = tile.shape[1], tile.shape[2]
    table = half_tables(side)
    tables = [jnp.asarray(split_table(table)), jnp.asarray(split_table(table.transpose(0, 2, 1)))]
    amps, probes = prepare(off, amp, probe)
    vmem = pl.BlockSpec(memory_space=pltpu.VMEM)
    shape = lambda *dims: jax.ShapeDtypeStruct(dims, F32)
    return pl.pallas_call(
        functools.partial(patches_kernel, scale=scale),
        grid=(count // together,),
        out_shape=(shape(2, rows, cols), shape(2, side, side), shape(2, rows - side, side),
                   shape(2, side // 2, cols), shape(2, side // 2, cols),
                   shape(2, side, side), shape(2, side, side)),
        in_specs=[pl.BlockSpec(memory_space=pltpu.SMEM)] + [vmem] * 8
                 + [pl.BlockSpec((together, 2, side, side), lambda i: (i, 0, 0, 0)),
                    pl.BlockSpec((together, 2, side, side // 2), lambda i: (i, 0, 0, 0))] + [vmem] * 2,
        out_specs=[vmem] * 7,
        scratch_shapes=[pltpu.VMEM((2, rows + side, cols + side), F32)] * 2
                     + [pltpu.VMEM((together, 2, side, side), F32)] + [pltpu.VMEM((together, 2, side, side), BF16)] * 4,
        compiler_params=pltpu.CompilerParams(vmem_limit_bytes=50 * 1024 * 1024),
    )(off, tile, upper, middle, lower, bottom, deeper, relayed, corner, probes, amps, *tables)


ACROSS, LINES = (2, 4, 6), (4, 8, 12)


def exchanged(pieces, distances, axis):
    return [lax.ppermute(piece, axis, [(i, i ^ distance) for i in range(lax.axis_size(axis))])
            for piece, distance in zip(pieces, distances)]


def added(parts):
    while len(parts) > 1:
        parts = [parts[i] + parts[i + 1] for i in range(0, len(parts), 2)]
    return parts[0]


def scattered(value, me, distances, axis):
    rows = value.shape[0] // 4
    pieces = [lax.dynamic_slice_in_dim(value, (me ^ place) * rows, rows, 0) for place in range(4)]
    return added(pieces[:1] + exchanged(pieces[1:], distances, axis))


def everywhere(value, distances, axis):
    return added([value] + exchanged([value] * 3, distances, axis))


def gathered(value, me, distances, axis):
    rows = value.shape[0]
    whole = jnp.zeros((rows * 4, value.shape[1]), value.dtype)
    for place, part in enumerate([value] + exchanged([value] * 3, distances, axis)):
        whole = lax.dynamic_update_slice_in_dim(whole, part, (me ^ place) * rows, 0)
    return whole


def halved(value, distance, axis):
    rows = value.shape[0] // 2
    upper = (lax.axis_index(axis) & distance) != 0
    low, high = value[:rows], value[rows:]
    got, = exchanged([jnp.where(upper, low, high)], (distance,), axis)
    return jnp.where(upper, high, low) + got


def doubled(value, distance, axis):
    upper = (lax.axis_index(axis) & distance) != 0
    got, = exchanged([value], (distance,), axis)
    return jnp.concatenate([jnp.where(upper, got, value), jnp.where(upper, value, got)], axis=0)


def round_ring(value, step):
    size = lax.axis_size("col")
    return lax.ppermute(value, "col", [(i, i // 4 * 4 + (i + step) % 4) for i in range(size)])


def summed_everywhere(value):
    shape = value.shape
    value = value.reshape(-1, shape[-1])
    chip = (lax.axis_index("row") >> 1) & 3
    value = halved(value, 1, "row")
    value = scattered(value, chip, ACROSS, "row")
    value = everywhere(value, LINES, "col")
    value = value + exchanged([value], (8,), "row")[0]
    value = everywhere(value, (1, 2, 3), "col")
    value = gathered(value, chip, ACROSS, "row")
    value = doubled(value, 1, "row")
    return value.reshape(shape)


def long_way(value):
    value = round_ring(value, 1)
    value = round_ring(value, 1)
    pairs = []
    for source in range(lax.axis_size("col")):
        line, place = source // 4, source % 4
        if place != 2:
            pairs.append((source, line * 4 + (place + 1) % 4))
        elif line > 0:
            pairs.append((source, line * 4 - 1))
    return lax.ppermute(value, "col", pairs)


def deeper_rows(value):
    count = lax.axis_size("row")
    half = count // 2
    relayed = lax.ppermute(value, "row", [(half, count - 2)])
    deeper = lax.ppermute(value, "row", [(i, i - 1) for i in range(1, count) if i != half])
    return deeper, lax.ppermute(relayed, "row", [(count - 2, half - 1)])


def deeper_returned(value):
    count = lax.axis_size("row")
    half = count // 2
    relayed = lax.ppermute(value, "row", [(half - 1, 1)])
    deeper = lax.ppermute(value, "row", [(i, i + 1) for i in range(count - 1) if i != half - 1])
    return deeper + lax.ppermute(relayed, "row", [(1, half)])


def shards_body(object_field, probe, amplitude, offsets):
    side = probe.shape[1]
    cut = object_field.shape[1] - side // 2
    lower = long_way(object_field[:, cut:, :side])
    upper = passed_along(object_field[:, :side, :side], "col", -1)
    middle = passed_along(object_field[:, side:cut, :side], "col", -1)
    bottom = passed_along(object_field[:, :side // 2, :], "row", -1)
    deeper, relayed = deeper_rows(object_field[:, side // 2:side, :])
    corner = passed_along(upper, "row", -1)
    count = amplitude.shape[2] * lax.axis_size("row") * lax.axis_size("col")
    main, upper, lower, bottom, deeper, corner, probe_acc = all_patches(
        offsets[0, 0], object_field, upper, middle, lower, bottom, deeper, relayed, corner, probe, amplitude[0, 0], 1.0 / count)
    corner_back = passed_along(corner, "row", 1)
    lower_back = passed_along(lower, "col", 1)
    bottom_back = passed_along(bottom, "row", 1)
    deeper_back = deeper_returned(deeper)
    upper_back = passed_along(upper + corner_back, "col", 1)
    probe_total = summed_everywhere(probe_acc)
    right_back = jnp.concatenate([upper_back, lower_back], axis=1)
    below = jnp.concatenate([bottom_back, deeper_back], axis=1)
    main = main.at[:, :side, :].add(below)
    object_grad = main.at[:, :, :side].add(right_back)
    return (object_grad, probe_total)


def solution(mesh):
    placed = (
        P(None, "row", "col"),
        P(),
        P("row", "col", None, None, None),
        P("row", "col", None, None),
    )
    return jax.shard_map(
        shards_body, mesh=mesh, in_specs=placed, out_specs=(P(None, "row", "col"), P()), check_vma=False
    )
```
